32 devices in a mesh: groups: 2 (over y), seq: 4 (over z), exp: 4 (over x, core).
Axes of the slice: x: 2, y: 2, z: 4, core: 2. Of those that a mesh axis runs over, the one named last changes fastest.
Arguments:
- residual: bfloat16 [1024, 6144], P(('groups', 'seq'), 'exp'), parts along dimension 0, may hold values from -6 to 6
- query_rows: bfloat16 [1024, 6144], P(('groups', 'seq'), 'exp'), parts along dimension 0, may hold values from -6 to 6
- key_rows: bfloat16 [1024, 6144], P(('groups', 'seq'), 'exp'), parts along dimension 0, may hold values from -6 to 6
- value_rows: bfloat16 [1024, 6144], P(('groups', 'seq'), 'exp'), parts along dimension 0, may hold values from -6 to 6
- log_decay: float32 [1024, 48], P(('groups', 'seq'), 'exp'), parts along dimension 0, may hold values from -0.8 to 0
- attn_gain: float32 [6144], P('exp'), may hold values from 0.1 to 1.9
- norm_gain: float32 [6144], P('exp'), may hold values from 0.1 to 1.9
- router: bfloat16 [6144, 32], P('exp'), may hold values from -0.3125 to 0.3125
- expert_ids: int32 [1024, 2], P(('groups', 'seq')), parts along dimension 0, may hold values from 0 to 31, all different within a row
- priority: int32 [8, 128], P(('groups', 'seq')), parts along dimension 0, may hold values from 0 to 127, each once within a row
- gate_weight: bfloat16 [4, 6144, 4608], P('exp', None, 'seq'), may hold values from -0.078125 to 0.078125
- up_weight: bfloat16 [4, 6144, 4608], P('exp', None, 'seq'), may hold values from -0.078125 to 0.078125
- down_weight: bfloat16 [4, 4608, 6144], P('exp', None, 'seq'), may hold values from -0.125 to 0.125
Outputs:
- layer_out: bfloat16 [1024, 6144], P(('groups', 'seq'), 'exp'), parts along dimension 0
The draws below stay inside these ranges and needn't reach their ends.
There are 2 independent parts, one for each index of `groups`. The reference program is written for one: setup_inputs(seed, part) draws one part's arguments, and reference() takes and returns one part's arrays. A program takes and returns all parts, laid end to end along the dimension named above; an argument that names none is the same for every part. Nothing has to cross between parts.
Inputs may be any that keep to these rules, and one draw needn't show every extreme that they name: `expert_ids`: each row names two different experts; ids of 4 or more name experts whose weights are not given. `priority`: each row holds every number from 0 to 127 once.
All inputs are finite; a program needn't handle non-finite values.
Results may differ from the reference program's by a relative error of at most 0.0047.
Values may be sent and summed in bfloat16 or wider, within the bound.
No kernel may reach another device: no remote copies, remote signals or barrier semaphores. Data moves between devices by JAX's collectives and lax.ppermute only.
A program may use at most 128 MiB of HBM per device.

```python
import math
import jax
import jax.numpy as jnp
from jax import lax

D = 6144
HEAD = 128
HEADS = 48
FF = 4608
EXPERTS = 32
TOP = 2
TOK_DEV = 128
TOKENS = 512
HELD = 4
CAP = 8
N_SEQ = 4


def draw_log_decay(key, part):
    streams = jax.random.split(jax.random.fold_in(key, 17), 5)
    share = 0.5
    fast = jax.random.uniform(streams[0], (HEADS,)) < share
    rough = jnp.exp(jax.random.uniform(streams[1], (TOKENS, HEADS), minval=-0.69, maxval=0.69))
    blocks = TOKENS // TOK_DEV
    blockwise = jnp.exp(jax.random.uniform(streams[2], (blocks, 1, HEADS), minval=-0.69, maxval=0.69))
    blockwise = jnp.broadcast_to(blockwise, (blocks, TOK_DEV, HEADS)).reshape(TOKENS, HEADS)
    slow_rate = 0.25 * math.log(10.0) / TOKENS
    rate = jnp.where(fast, 1.0 / 40.0, slow_rate)[None, :] * rough * blockwise
    places = jax.random.randint(streams[3], (4,), 0, TOKENS)
    bursty = jnp.any(jnp.arange(TOKENS)[:, None] == places[None, :], axis=1)
    loss = jax.random.uniform(streams[4], (HEADS,), minval=0.2, maxval=0.5)
    jump = jnp.where(bursty[:, None] & jnp.logical_not(fast)[None, :], jnp.log(1.0 - loss)[None, :], 0.0)
    return (jump - rate).astype(jnp.float32)


def raised(array, own_key, source, target, parts, factor):
    def block_of(dim):
        return (jnp.arange(array.shape[dim]) // (array.shape[dim] // parts)).reshape((-1,) + (1,) * (array.ndim - 1 - dim))

    first = jax.random.permutation(own_key, parts)[block_of(target)]
    second = (block_of(target) + parts // 2) % parts
    return jnp.where((block_of(source) == first) | (block_of(source) == second), factor * array, array)


def shard_levels(stream_key, extent, pieces, low, high):
    gain = 1.0
    for axis_at, parts in pieces:
        draws = jax.random.uniform(jax.random.fold_in(jax.random.fold_in(stream_key, 6), axis_at), (parts,), jnp.float32, low / len(pieces), high / len(pieces))
        gain = gain * jnp.repeat(jnp.exp(draws), extent[axis_at] // parts).reshape((-1,) + (1,) * (len(extent) - 1 - axis_at))
    return gain


def choose_distinct(rng, rows, number_of, top, lift):
    ranking = jax.random.permutation(jax.random.fold_in(rng, 1), number_of)
    favour = ranking
    for power in range(3):
        favour = favour * favour // number_of
    favour = favour * lift // number_of
    tickets = jax.random.randint(jax.random.fold_in(rng, 2), (rows, number_of), 0, 4096) + favour
    fixed_rows = jax.random.permutation(jax.random.fold_in(rng, 3), rows)[jnp.arange(number_of) % rows]
    tickets = jnp.where(jnp.arange(rows)[:, None] == fixed_rows[None, :], 1 << 14, tickets)
    score = tickets * number_of + jnp.arange(number_of)
    return lax.top_k(score.astype(jnp.int32), top)[1].astype(jnp.int32)


def gaussian(stream_key, extent, scale, reach, shards=(), kind=jnp.bfloat16):
    array = scale * jax.random.normal(stream_key, extent, jnp.float32)
    if shards:
        array = array * shard_levels(stream_key, extent, shards, -0.22, 0.18)
    return jnp.clip(array, -reach, reach).astype(kind)


def gaussian_with(stream_key, dims, width, bound, cuts, heavy, held_as=jnp.bfloat16):
    array = width * jax.random.normal(stream_key, dims, jnp.float32)
    if cuts:
        array = array * shard_levels(stream_key, dims, cuts, -0.22, 0.18)
    return jnp.clip(raised(array, jax.random.fold_in(stream_key, 3), *heavy), -bound, bound).astype(held_as)


def setup_inputs(seed: int = 0, part: int = 0) -> dict:
    arg_keys = jax.random.split(jax.random.key(seed), 14)
    own_keys = jax.random.split(jax.random.fold_in(arg_keys[13], part), 14)
    return {
        "residual": gaussian(own_keys[0], (TOKENS, D), 1.0, 6.0, ((0, 4), (1, 4))),
        "query_rows": gaussian(own_keys[1], (TOKENS, D), 1.0, 6.0, ((0, 4), (1, 4))),
        "key_rows": gaussian(own_keys[2], (TOKENS, D), 1.0, 6.0, ((0, 4), (1, 4))),
        "value_rows": gaussian(own_keys[3], (TOKENS, D), 1.0, 6.0, ((0, 4), (1, 4))),
        "log_decay": draw_log_decay(jax.random.fold_in(jax.random.fold_in(arg_keys[13], part), 71), part),
        "attn_gain": jnp.clip(1.0 + 0.18 * jax.random.normal(arg_keys[5], (D,), jnp.float32), 0.1, 1.9),
        "norm_gain": jnp.clip(1.0 + 0.18 * jax.random.normal(arg_keys[6], (D,), jnp.float32), 0.1, 1.9),
        "router": gaussian(arg_keys[7], (D, EXPERTS), (D // 16) ** -0.5, 0.3125, ((0, 4),)),
        "expert_ids": choose_distinct(own_keys[8], TOKENS, EXPERTS, TOP, 512),
        "priority": jax.vmap(lambda own: jax.random.permutation(own, TOK_DEV))(jax.random.split(own_keys[9], N_SEQ)).reshape((N_SEQ, TOK_DEV)).astype(jnp.int32),
        "gate_weight": gaussian(arg_keys[10], (HELD, D, FF), D ** -0.5, 0.078125, ((0, 4), (2, 4))),
        "up_weight": gaussian(arg_keys[11], (HELD, D, FF), D ** -0.5, 0.078125, ((0, 4), (2, 4))),
        "down_weight": gaussian_with(arg_keys[12], (HELD, FF, D), FF ** -0.5, 0.125, ((0, 4), (2, 4)), (1, 2, 4, 2.0)),
    }


def block_local(inputs):
    queries, keys, values, cumulative = inputs
    rows = queries.shape[0]
    scores = jnp.einsum('thd,shd->hts', queries.astype(jnp.float32), keys.astype(jnp.float32))
    causal = (jnp.arange(rows)[:, None] >= jnp.arange(rows)[None, :])[None]
    spread = cumulative.T[:, :, None] - cumulative.T[:, None, :]
    weights = jnp.where(causal, scores * jnp.exp(jnp.where(causal, spread, 0.0)), 0.0).astype(jnp.bfloat16)
    local_part = jnp.einsum('hts,shd->thd', weights.astype(jnp.float32), values.astype(jnp.float32))
    to_end = jnp.exp(cumulative[-1][None, :] - cumulative)
    keyed = (keys.astype(jnp.float32) * to_end[:, :, None]).astype(jnp.bfloat16)
    state = jnp.einsum('thd,the->hde', keyed.astype(jnp.float32), values.astype(jnp.float32))
    return (local_part, state, jnp.exp(cumulative[-1]))

def reference(residual, query_rows, key_rows, value_rows, log_decay, attn_gain, norm_gain, router, expert_ids, priority, gate_weight, up_weight, down_weight):
    blocks = TOKENS // TOK_DEV
    queries = query_rows.reshape(blocks, TOK_DEV, HEADS, HEAD)
    keys = key_rows.reshape(blocks, TOK_DEV, HEADS, HEAD)
    values = value_rows.reshape(blocks, TOK_DEV, HEADS, HEAD)
    cumulative = jnp.cumsum(log_decay.reshape(blocks, TOK_DEV, HEADS), axis=1)
    local_part, states, decays = lax.map(block_local, (queries, keys, values, cumulative))

    def advance(carry, inputs):
        state, decay = inputs
        return (decay[:, None, None] * carry + state, carry)
    start = jnp.zeros((HEADS, HEAD, HEAD), jnp.float32)
    _, carried = lax.scan(advance, start, (states, decays))
    inter = jnp.einsum('bthd,bhde->bthe', queries.astype(jnp.float32), carried, precision=lax.Precision.HIGHEST)
    attended = local_part + jnp.exp(cumulative)[:, :, :, None] * inter
    normed = attended * lax.rsqrt(lax.optimization_barrier(jnp.mean(attended * attended, axis=-1, keepdims=True)) + 1e-06)
    normed = normed * attn_gain.reshape(HEADS, HEAD)
    mixed = (residual.astype(jnp.float32) + normed.reshape(TOKENS, D)).astype(jnp.bfloat16)
    mixed_f = mixed.astype(jnp.float32)
    inverse = lax.rsqrt(lax.optimization_barrier(jnp.sum(mixed_f * mixed_f, axis=1)) / D + 1e-06)
    scaled = mixed_f * norm_gain * inverse[:, None]
    tokens_in = scaled.astype(jnp.bfloat16)
    logits = jnp.dot(scaled, router.astype(jnp.float32), precision=lax.Precision.HIGHEST)
    probs = jax.nn.sigmoid(logits)
    chosen = expert_ids[:, :, None] == jnp.arange(EXPERTS, dtype=jnp.int32)[None, None, :]
    selected = lax.optimization_barrier(jnp.sum(jnp.where(chosen, probs[:, None, :], 0.0), axis=-1))
    gates = selected / lax.optimization_barrier(jnp.sum(selected, axis=-1, keepdims=True))
    is_held = expert_ids[:, :, None] == jnp.arange(HELD, dtype=jnp.int32)[None, None, :]
    member = jnp.where(jnp.any(is_held, axis=1), 1.0, 0.0).astype(jnp.float32)
    gate_held = lax.optimization_barrier(jnp.sum(jnp.where(is_held, gates[:, :, None], 0.0), axis=1))
    earlier = jnp.where(priority[:, None, :] < priority[:, :, None], 1.0, 0.0).astype(jnp.float32)
    member_b = member.reshape(blocks, TOK_DEV, HELD)
    rank = jnp.einsum('bts,bse->bte', earlier, member_b)
    kept = (member_b > 0.5) & (rank < CAP)
    slot_ids = jnp.arange(CAP).astype(rank.dtype)
    place = kept.transpose(0, 2, 1)[:, :, None, :] & (rank.transpose(0, 2, 1)[:, :, None, :] == slot_ids[None, None, :, None])
    place_f = jnp.where(place, 1.0, 0.0).astype(jnp.float32)
    buffers = jnp.einsum('bect,btd->ebcd', place_f, tokens_in.reshape(blocks, TOK_DEV, D).astype(jnp.float32)).astype(jnp.bfloat16)

    def run_expert(inputs):
        slots, gate_w, up_w, down_w = inputs
        rows = slots.reshape(blocks * CAP, D)
        gate = jnp.dot(rows, gate_w, preferred_element_type=jnp.float32)
        up = jnp.dot(rows, up_w, preferred_element_type=jnp.float32)
        hidden = (jax.nn.silu(gate) * up).astype(jnp.bfloat16)
        return jnp.dot(hidden, down_w, preferred_element_type=jnp.float32).astype(jnp.bfloat16)
    expert_out = lax.map(run_expert, (buffers, gate_weight, up_weight, down_weight))
    expert_out = expert_out.reshape(HELD, blocks, CAP, D).astype(jnp.float32)
    weighted = place_f * gate_held.reshape(blocks, TOK_DEV, HELD).transpose(0, 2, 1)[:, :, None, :]
    combined = jnp.einsum('bect,ebcd->btd', weighted, expert_out, precision=lax.Precision.HIGHEST)
    return (mixed_f + combined.reshape(TOKENS, D)).astype(jnp.bfloat16)
```

```python
import functools

import jax
import jax.numpy as jnp
from jax import lax
from jax.experimental import pallas as pl
from jax.experimental.pallas import tpu as pltpu
from jax.sharding import PartitionSpec as P

HEAD = 128
LANES = 128
CAP = 8
PAD = 16
EPS = 1e-06
F32 = jnp.float32
BF16 = jnp.bfloat16

VMEM = pl.BlockSpec(memory_space=pltpu.VMEM)


def nt(a, b):
    return lax.dot_general(a, b, (((1,), (1,)), ((), ())), preferred_element_type=F32)


def tn(a, b):
    return lax.dot_general(a, b, (((0,), (0,)), ((), ())), preferred_element_type=F32)


def nn(a, b):
    return lax.dot_general(a, b, (((1,), (0,)), ((), ())), preferred_element_type=F32)


def iota(shape, dim):
    return lax.broadcasted_iota(jnp.int32, shape, dim)


def split_hi_lo(x):
    hi = x.astype(BF16)
    return hi, (x - hi.astype(F32)).astype(BF16)


def state_kernel(heads, shares, share_rows, k_ref, v_ref, decay_ref, pay_ref, row_ref, col_ref, pad_ref):
    rows = k_ref.shape[0]
    pad_ref[...] = jnp.zeros_like(pad_ref)
    pad_ref[0:heads, :] = decay_ref[...]
    log_decay = pad_ref[...]
    lower = jnp.where(iota((rows, rows), 0) >= iota((rows, rows), 1), 1.0, 0.0).astype(F32)
    cum_col = lax.dot_general(
        lower, log_decay, (((1,), (1,)), ((), ())), precision=lax.Precision.HIGHEST, preferred_element_type=F32
    )
    cum_row = lax.dot_general(
        log_decay, lower, (((1,), (1,)), ((), ())), precision=lax.Precision.HIGHEST, preferred_element_type=F32
    )
    row_ref[...] = cum_row
    col_ref[...] = cum_col
    to_end = jnp.exp(cum_col[rows - 1 : rows, :] - cum_col)
    hi, lo = split_hi_lo(jnp.exp(cum_col[rows - 1 : rows, :]))
    for s in range(shares):
        pay_ref[s, share_rows : share_rows + PAD, :] = jnp.concatenate(
            [jnp.broadcast_to(hi, (8, LANES)), jnp.broadcast_to(lo, (8, LANES))], axis=0
        )
    for h in range(heads):
        cols = slice(h * HEAD, (h + 1) * HEAD)
        keyed = (k_ref[:, cols].astype(F32) * to_end[:, h : h + 1]).astype(BF16)
        state = tn(keyed, v_ref[:, cols]).astype(BF16)
        at = h * HEAD
        while at < (h + 1) * HEAD:
            share, inner = divmod(at, share_rows)
            take = min(share_rows - inner, (h + 1) * HEAD - at)
            pay_ref[share, inner : inner + take, :] = state[at - h * HEAD : at - h * HEAD + take, :]
            at += take


def local_kernel(heads, q_ref, k_ref, v_ref, row_ref, col_ref, out_ref):
    rows = q_ref.shape[0]
    causal = iota((rows, rows), 0) >= iota((rows, rows), 1)
    for h in range(heads):
        cols = slice(h * HEAD, (h + 1) * HEAD)
        scores = nt(q_ref[:, cols], k_ref[:, cols])
        spread = col_ref[:, h : h + 1] - row_ref[h : h + 1, :]
        weights = jnp.where(causal, scores * jnp.exp(jnp.where(causal, spread, 0.0)), 0.0).astype(BF16)
        out_ref[:, cols] = nn(weights, v_ref[:, cols])


def place_kernel(held, ids_ref, prio_ref, place_ref):
    rows = ids_ref.shape[1]
    order = prio_ref[...].astype(F32)
    across = jnp.broadcast_to(order, (rows, rows))
    earlier = jnp.where(across.T < across, 1.0, 0.0).astype(BF16)
    ids = ids_ref[...]
    expert = iota((8 * pl.cdiv(held, 8), rows), 0)
    hit = expert == ids[0:1, :]
    for i in range(1, ids.shape[0]):
        hit = hit | (expert == ids[i : i + 1, :])
    member = jnp.where(hit, 1.0, 0.0)
    rank = nn(member.astype(BF16), earlier)
    slot = iota((CAP, rows), 0).astype(F32)
    for e in range(held):
        chosen = (member[e : e + 1, :] > 0.5) & (rank[e : e + 1, :] == slot)
        place_ref[e * CAP : (e + 1) * CAP, :] = jnp.where(chosen, 1.0, 0.0)


def scan_kernel(shares, share_rows, in_ref, out_ref):
    me = lax.axis_index("seq")
    row = me * share_rows + iota((share_rows, LANES), 0)
    onehot = jnp.where(row // HEAD == iota((share_rows, LANES), 1), 1.0, 0.0)
    carry = jnp.zeros((share_rows, LANES), F32)
    for b in range(shares):
        out_ref[b, :, :] = carry.astype(BF16)
        if b + 1 < shares:
            tail = in_ref[b, share_rows : share_rows + PAD, :].astype(F32)
            decay = tail[0:1, :] + tail[8:9, :]
            each = jnp.sum(onehot * decay, axis=1, keepdims=True)
            carry = each * carry + in_ref[b, 0:share_rows, :].astype(F32)


def mix_kernel(
    heads, held, copies, q_ref, local_ref, carried_ref, col_ref, res_ref, again_ref, ngain_ref, router_ref, place_ref,
    mixed_ref, slots_ref, stats_ref,
):
    rows = q_ref.shape[0]
    width = heads * HEAD
    experts = router_ref.shape[0]
    place = place_ref[...].astype(BF16)
    grow = jnp.exp(col_ref[...])
    squares = jnp.zeros((rows, 1), F32)
    picked_squares = jnp.zeros((held * CAP, 1), F32)
    logits = jnp.zeros((experts, rows), F32)
    for h in range(heads):
        cols = slice(h * HEAD, (h + 1) * HEAD)
        inter = nn(q_ref[:, cols], carried_ref[h * HEAD : (h + 1) * HEAD, :])
        attended = local_ref[:, cols] + grow[:, h : h + 1] * inter
        power = jnp.mean(attended * attended, axis=1, keepdims=True)
        normed = attended * lax.rsqrt(power + EPS) * again_ref[:, cols]
        mixed = (res_ref[:, cols].astype(F32) + normed).astype(BF16)
        mixed_ref[:, cols] = mixed
        mixed_f = mixed.astype(F32)
        squares += jnp.sum(mixed_f * mixed_f, axis=1, keepdims=True)
        hi, lo = split_hi_lo(mixed_f * ngain_ref[:, cols])
        logits += nt(router_ref[:, cols], hi) + nt(router_ref[:, cols], lo)
        picked = nn(place, mixed)
        picked_squares += jnp.sum(picked * picked, axis=1, keepdims=True)
        sent = (picked * ngain_ref[:, cols]).astype(BF16)
        for s in range(copies):
            for e in range(held):
                slots_ref[s, e, :, cols] = sent[e * CAP : (e + 1) * CAP, :]
    lane = iota((held * CAP, LANES), 1)
    hi, lo = split_hi_lo(picked_squares)
    extra = jnp.where(lane == 0, hi.astype(F32), jnp.where(lane == 1, lo.astype(F32), 0.0)).astype(BF16)
    for s in range(copies):
        for e in range(held):
            slots_ref[s, e, :, width : width + LANES] = extra[e * CAP : (e + 1) * CAP, :]
    stats_ref[0:experts, :] = logits
    stats_ref[experts : experts + 8, :] = jnp.broadcast_to(squares, (rows, rows)).T[0:8, :]


def gate_up_kernel(seqs, held, width, chunk, in_ref, gate_ref, up_ref, out_ref, x_ref, acc_g, acc_u):
    step = pl.program_id(0)
    per = width // chunk

    @pl.when(step == 0)
    def _():
        for s in range(seqs):
            for k in range(held):
                for p in range(per):
                    x_ref[k * per + p, s * CAP : (s + 1) * CAP, :] = in_ref[s * held + k, :, p * chunk : (p + 1) * chunk]
        acc_g[...] = jnp.zeros_like(acc_g)
        acc_u[...] = jnp.zeros_like(acc_u)

    x = x_ref[step]
    acc_g[...] += nn(x, gate_ref[0])
    acc_u[...] += nn(x, up_ref[0])

    @pl.when(step == pl.num_programs(0) - 1)
    def _():
        parts = []
        for s in range(seqs):
            total = jnp.zeros((CAP, 1), F32)
            for k in range(held):
                tail = in_ref[s * held + k, :, width : width + LANES].astype(F32)
                total += tail[:, 0:1] + tail[:, 1:2]
            parts.append(total)
        squares = jnp.concatenate(parts, axis=0)
        inverse = lax.rsqrt(squares / (held * width) + EPS)
        gate = acc_g[...] * inverse
        up = acc_u[...] * inverse
        out_ref[...] = (gate * (1.0 / (1.0 + jnp.exp(-gate))) * up).astype(BF16)


def down_kernel(seqs, order_ref, h_ref, w_ref, out_ref, acc):
    step = pl.program_id(0)

    @pl.when(step == 0)
    def _():
        acc[...] = jnp.zeros_like(acc)

    acc[...] += nn(h_ref[0], w_ref[0])

    @pl.when(step == pl.num_programs(0) - 1)
    def _():
        for s in range(seqs):
            out_ref[s, :, :] = acc[s * CAP : (s + 1) * CAP, :].astype(BF16)


def gates_kernel(held, total_width, parts, *refs):
    stats_refs, (ids_ref, place_ref, hi_ref, lo_ref) = refs[:parts], refs[parts:]
    total = stats_refs[0][...]
    for ref in stats_refs[1:]:
        total = total + ref[...]
    experts = total.shape[0] - 8
    inverse = lax.rsqrt(total[experts : experts + 1, :] / total_width + EPS)
    logits = total[0:experts, :] * inverse
    probs = 1.0 / (1.0 + jnp.exp(-logits))
    expert = iota(probs.shape, 0)
    ids = ids_ref[...]
    chosen = [
        jnp.sum(jnp.where(expert == ids[i : i + 1, :], probs, 0.0), axis=0, keepdims=True) for i in range(ids.shape[0])
    ]
    norm = chosen[0]
    for c in chosen[1:]:
        norm = norm + c
    for e in range(held):
        gate = jnp.zeros_like(norm)
        for i, c in enumerate(chosen):
            gate += jnp.where(ids[i : i + 1, :] == e, c / norm, 0.0)
        hi, lo = split_hi_lo(place_ref[e * CAP : (e + 1) * CAP, :] * gate)
        hi_ref[e * CAP : (e + 1) * CAP, :] = hi.astype(F32)
        lo_ref[e * CAP : (e + 1) * CAP, :] = lo.astype(F32)


def combine_kernel(held, mixed_ref, hi_ref, lo_ref, *refs):
    y_refs, out_ref = refs[:-1], refs[-1]
    if len(y_refs) > 1:
        y = jnp.concatenate([r[...].astype(F32) for r in y_refs], axis=0).astype(BF16)
    else:
        y = jnp.concatenate([y_refs[0][e].astype(F32) for e in range(held)], axis=0).astype(BF16)
    extra = tn(hi_ref[...].astype(BF16), y) + tn(lo_ref[...].astype(BF16), y)
    out_ref[...] = (mixed_ref[...].astype(F32) + extra).astype(BF16)


def call(body, out_shape, args, name, scratch=(), flops=0, nbytes=0):
    return pl.pallas_call(
        body,
        out_shape=out_shape,
        in_specs=[VMEM] * len(args),
        out_specs=jax.tree.map(lambda _: VMEM, out_shape),
        scratch_shapes=list(scratch),
        name=name,
        cost_estimate=pl.CostEstimate(flops=flops or 1000, bytes_accessed=nbytes or 1000, transcendentals=0),
    )(*args)


def shaped(shape, dtype):
    return jax.ShapeDtypeStruct(shape, dtype)


def body(
    residual, query_rows, key_rows, value_rows, log_decay, attn_gain, norm_gain, router, expert_ids, priority,
    gate_weight, up_weight, down_weight,
):
    rows, width = residual.shape
    heads = width // HEAD
    held = lax.axis_size("exp")
    seqs = lax.axis_size("seq")
    experts = router.shape[1]
    share_rows = width // seqs
    hidden_part = gate_weight.shape[2]
    out_part = down_weight.shape[2]
    ids = expert_ids.T
    payload, cum_row, cum_col = call(
        functools.partial(state_kernel, heads, seqs, share_rows),
        (
            shaped((seqs, share_rows + PAD, LANES), BF16),
            shaped((LANES, rows), F32),
            shaped((rows, LANES), F32),
        ),
        (key_rows, value_rows, log_decay.T),
        "state",
        scratch=[pltpu.VMEM((LANES, rows), F32)],
        flops=60_000_000,
        nbytes=1_200_000,
    )
    arrived = lax.all_to_all(payload, "seq", split_axis=0, concat_axis=0, tiled=True)
    local = call(
        functools.partial(local_kernel, heads),
        shaped((rows, width), F32),
        (query_rows, key_rows, value_rows, cum_row, cum_col),
        "local",
        flops=200_000_000,
        nbytes=2_000_000,
    )
    place = call(
        functools.partial(place_kernel, held),
        shaped((held * CAP, rows), F32),
        (ids, priority),
        "place",
    )
    prefix = call(
        functools.partial(scan_kernel, seqs, share_rows),
        shaped((seqs, share_rows, LANES), BF16),
        (arrived,),
        "scan",
    )
    carried = lax.all_to_all(prefix, "seq", split_axis=0, concat_axis=0, tiled=True).reshape(width, LANES)
    mixed, slots, stats = call(
        functools.partial(mix_kernel, heads, held, seqs),
        (
            shaped((rows, width), BF16),
            shaped((seqs, held, CAP, width + LANES), BF16),
            shaped((experts + 8, rows), F32),
        ),
        (
            query_rows, local, carried, cum_col, residual, attn_gain[None], norm_gain[None], router.T, place,
        ),
        "mix",
        flops=200_000_000,
        nbytes=3_000_000,
    )
    slots = slots.reshape(seqs * held, CAP, width + LANES)
    gathered = lax.all_to_all(slots, ("seq", "exp"), split_axis=0, concat_axis=0, tiled=True)
    stat_parts = [stats]
    for r in range(1, held):
        stat_parts.append(lax.ppermute(stats, "exp", [(i, (i + r) % held) for i in range(held)]))
    slot_rows = seqs * CAP
    chunk = width // 2
    hidden = pl.pallas_call(
        functools.partial(gate_up_kernel, seqs, held, width, chunk),
        out_shape=shaped((slot_rows, hidden_part), BF16),
        grid=(held * width // chunk,),
        in_specs=[
            VMEM,
            pl.BlockSpec((1, chunk, hidden_part), lambda i: (0, i, 0)),
            pl.BlockSpec((1, chunk, hidden_part), lambda i: (0, i, 0)),
        ],
        out_specs=pl.BlockSpec((slot_rows, hidden_part), lambda i: (0, 0)),
        scratch_shapes=[
            pltpu.VMEM((held * width // chunk, slot_rows, chunk), BF16),
            pltpu.VMEM((slot_rows, hidden_part), F32),
            pltpu.VMEM((slot_rows, hidden_part), F32),
        ],
        name="gate_up",
        cost_estimate=pl.CostEstimate(flops=900_000_000, bytes_accessed=28_000_000, transcendentals=0),
    )(gathered, gate_weight, up_weight)
    me = lax.axis_index("seq")
    if seqs <= 8:
        parts = [hidden]
        for r in range(1, seqs):
            parts.append(lax.ppermute(hidden, "seq", [(i, (i + r) % seqs) for i in range(seqs)]))
        whole = jnp.stack(parts)
        order = jnp.mod(me - jnp.arange(seqs, dtype=jnp.int32), seqs)
    else:
        whole = lax.all_gather(hidden, "seq", axis=0)
        order = jnp.arange(seqs, dtype=jnp.int32)
    expert_out = pl.pallas_call(
        functools.partial(down_kernel, seqs),
        out_shape=shaped((seqs, CAP, out_part), BF16),
        grid_spec=pltpu.PrefetchScalarGridSpec(
            num_scalar_prefetch=1,
            grid=(seqs,),
            in_specs=[
                pl.BlockSpec((1, slot_rows, hidden_part), lambda i, o: (i, 0, 0)),
                pl.BlockSpec((1, hidden_part, out_part), lambda i, o: (0, o[i], 0)),
            ],
            out_specs=pl.BlockSpec((seqs, CAP, out_part), lambda i, o: (0, 0, 0)),
            scratch_shapes=[pltpu.VMEM((slot_rows, out_part), F32)],
        ),
        name="down",
        cost_estimate=pl.CostEstimate(flops=450_000_000, bytes_accessed=14_000_000, transcendentals=0),
    )(order, whole, down_weight)
    if seqs == held:
        pieces = []
        for r in range(seqs):
            target = [
                (s * held + e, ((e + r) % seqs) * held + s) for s in range(seqs) for e in range(held)
            ]
            mine = lax.dynamic_index_in_dim(
                expert_out, jnp.mod(lax.axis_index("exp") + r, seqs), axis=0, keepdims=False
            )
            pieces.append(lax.ppermute(mine, ("seq", "exp"), target))
        stacked = jnp.stack(pieces)
        source = jnp.mod(me - jnp.arange(held, dtype=jnp.int32), held)
        y = (jnp.take(stacked, source, axis=0),)
    else:
        returned = lax.all_to_all(expert_out, "seq", split_axis=0, concat_axis=1, tiled=True)
        returned = returned.reshape(CAP, seqs * out_part)
        y = (lax.all_to_all(returned[None], "exp", split_axis=2, concat_axis=0, tiled=True),)
    hi, lo = call(
        functools.partial(gates_kernel, held, held * width, len(stat_parts)),
        (shaped((held * CAP, rows), F32),) * 2,
        (*stat_parts, ids, place),
        "gates",
    )
    return call(
        functools.partial(combine_kernel, held),
        shaped((rows, width), BF16),
        (mixed, hi, lo, *y),
        "combine",
    )


def solution(mesh):
    token = P(("groups", "seq"), "exp")
    return jax.shard_map(
        body,
        mesh=mesh,
        in_specs=(
            token, token, token, token, token, P("exp"), P("exp"), P("exp", None),
            P(("groups", "seq"), None), P(("groups", "seq"), None),
            P("exp", None, "seq"), P("exp", None, "seq"), P("exp", None, "seq"),
        ),
        out_specs=token,
        check_vma=False,
    )
```

```python
import functools

import jax
import jax.numpy as jnp
from jax import lax
from jax.experimental import pallas as pl
from jax.experimental.pallas import tpu as pltpu
from jax.sharding import PartitionSpec as P


HEAD = 128
LANES = 128
CAP = 8
PAD = 16
EPS = 1e-06
SMALL = 8 << 20
F32 = jnp.float32
BF16 = jnp.bfloat16


VMEM = pl.BlockSpec(memory_space=pltpu.VMEM)


def nt(a, b):
    return lax.dot_general(a, b, (((1,), (1,)), ((), ())), preferred_element_type=F32)


def tn(a, b):
    return lax.dot_general(a, b, (((0,), (0,)), ((), ())), preferred_element_type=F32)


def nn(a, b):
    return lax.dot_general(a, b, (((1,), (0,)), ((), ())), preferred_element_type=F32)


def iota(shape, dim):
    return lax.broadcasted_iota(jnp.int32, shape, dim)


def split_hi_lo(x):
    hi = x.astype(BF16)
    return hi, (x - hi.astype(F32)).astype(BF16)


def state_kernel(heads, shares, share_rows, k_ref, v_ref, decay_ref, pay_ref, row_ref, col_ref, pad_ref):
    rows = k_ref.shape[0]
    pad_ref[...] = jnp.zeros_like(pad_ref)
    pad_ref[0:heads, :] = decay_ref[...]
    log_decay = pad_ref[...]
    lower = jnp.where(iota((rows, rows), 0) >= iota((rows, rows), 1), 1.0, 0.0).astype(F32)
    cum_col = lax.dot_general(
        lower, log_decay, (((1,), (1,)), ((), ())), precision=lax.Precision.HIGHEST, preferred_element_type=F32
    )
    cum_row = lax.dot_general(
        log_decay, lower, (((1,), (1,)), ((), ())), precision=lax.Precision.HIGHEST, preferred_element_type=F32
    )
    row_ref[...] = cum_row
    col_ref[...] = cum_col
    to_end = jnp.exp(cum_col[rows - 1 : rows, :] - cum_col)
    hi, lo = split_hi_lo(jnp.exp(cum_col[rows - 1 : rows, :]))
    for s in range(shares):
        pay_ref[s, share_rows : share_rows + PAD, :] = jnp.concatenate(
            [jnp.broadcast_to(hi, (8, LANES)), jnp.broadcast_to(lo, (8, LANES))], axis=0
        )
    for h in range(heads):
        cols = slice(h * HEAD, (h + 1) * HEAD)
        keyed = (k_ref[:, cols].astype(F32) * to_end[:, h : h + 1]).astype(BF16)
        state = tn(keyed, v_ref[:, cols]).astype(BF16)
        at = h * HEAD
        while at < (h + 1) * HEAD:
            share, inner = divmod(at, share_rows)
            take = min(share_rows - inner, (h + 1) * HEAD - at)
            pay_ref[share, inner : inner + take, :] = state[at - h * HEAD : at - h * HEAD + take, :]
            at += take


def local_kernel(heads, q_ref, k_ref, v_ref, row_ref, col_ref, out_ref):
    rows = q_ref.shape[0]
    causal = iota((rows, rows), 0) >= iota((rows, rows), 1)
    for h in range(heads):
        cols = slice(h * HEAD, (h + 1) * HEAD)
        scores = nt(q_ref[:, cols], k_ref[:, cols])
        spread = col_ref[:, h : h + 1] - row_ref[h : h + 1, :]
        weights = jnp.where(causal, scores * jnp.exp(jnp.where(causal, spread, 0.0)), 0.0).astype(BF16)
        out_ref[:, cols] = nn(weights, v_ref[:, cols])


def place_kernel(held, ids_ref, prio_ref, place_ref):
    rows = ids_ref.shape[1]
    order = prio_ref[...].astype(F32)
    across = jnp.broadcast_to(order, (rows, rows))
    earlier = jnp.where(across.T < across, 1.0, 0.0).astype(BF16)
    ids = ids_ref[...]
    expert = iota((8 * pl.cdiv(held, 8), rows), 0)
    hit = expert == ids[0:1, :]
    for i in range(1, ids.shape[0]):
        hit = hit | (expert == ids[i : i + 1, :])
    member = jnp.where(hit, 1.0, 0.0)
    rank = nn(member.astype(BF16), earlier)
    slot = iota((CAP, rows), 0).astype(F32)
    for e in range(held):
        chosen = (member[e : e + 1, :] > 0.5) & (rank[e : e + 1, :] == slot)
        place_ref[e * CAP : (e + 1) * CAP, :] = jnp.where(chosen, 1.0, 0.0)


def scan_kernel(shares, share_rows, in_ref, out_ref):
    me = lax.axis_index("seq")
    row = me * share_rows + iota((share_rows, LANES), 0)
    onehot = jnp.where(row // HEAD == iota((share_rows, LANES), 1), 1.0, 0.0)
    carry = jnp.zeros((share_rows, LANES), F32)
    for b in range(shares):
        out_ref[b, :, :] = carry.astype(BF16)
        if b + 1 < shares:
            tail = in_ref[b, share_rows : share_rows + PAD, :].astype(F32)
            decay = tail[0:1, :] + tail[8:9, :]
            each = jnp.sum(onehot * decay, axis=1, keepdims=True)
            carry = each * carry + in_ref[b, 0:share_rows, :].astype(F32)


def mix_kernel(
    heads, held, copies, q_ref, local_ref, carried_ref, col_ref, res_ref, again_ref, ngain_ref, router_ref, place_ref,
    mixed_ref, slots_ref, stats_ref,
):
    rows = q_ref.shape[0]
    width = heads * HEAD
    experts = router_ref.shape[0]
    place = place_ref[...].astype(BF16)
    grow = jnp.exp(col_ref[...])
    squares = jnp.zeros((rows, 1), F32)
    picked_squares = jnp.zeros((held * CAP, 1), F32)
    logits = jnp.zeros((experts, rows), F32)
    for h in range(heads):
        cols = slice(h * HEAD, (h + 1) * HEAD)
        inter = nn(q_ref[:, cols], carried_ref[h * HEAD : (h + 1) * HEAD, :])
        attended = local_ref[:, cols] + grow[:, h : h + 1] * inter
        power = jnp.mean(attended * attended, axis=1, keepdims=True)
        normed = attended * lax.rsqrt(power + EPS) * again_ref[:, cols]
        mixed = (res_ref[:, cols].astype(F32) + normed).astype(BF16)
        mixed_ref[:, cols] = mixed
        mixed_f = mixed.astype(F32)
        squares += jnp.sum(mixed_f * mixed_f, axis=1, keepdims=True)
        hi, lo = split_hi_lo(mixed_f * ngain_ref[:, cols])
        logits += nt(router_ref[:, cols], hi) + nt(router_ref[:, cols], lo)
        picked = nn(place, mixed)
        picked_squares += jnp.sum(picked * picked, axis=1, keepdims=True)
        sent = (picked * ngain_ref[:, cols]).astype(BF16)
        for s in range(copies):
            for e in range(held):
                slots_ref[s, e, :, cols] = sent[e * CAP : (e + 1) * CAP, :]
    lane = iota((held * CAP, LANES), 1)
    hi, lo = split_hi_lo(picked_squares)
    extra = jnp.where(lane == 0, hi.astype(F32), jnp.where(lane == 1, lo.astype(F32), 0.0)).astype(BF16)
    for s in range(copies):
        for e in range(held):
            slots_ref[s, e, :, width : width + LANES] = extra[e * CAP : (e + 1) * CAP, :]
    stats_ref[0:experts, :] = logits
    stats_ref[experts : experts + 8, :] = jnp.broadcast_to(squares, (rows, rows)).T[0:8, :]


def gate_up_kernel(seqs, held, width, chunk, in_ref, gate_ref, up_ref, out_ref, x_ref, acc_g, acc_u):
    step = pl.program_id(0)
    per = width // chunk

    @pl.when(step == 0)
    def _():
        for s in range(seqs):
            for k in range(held):
                for p in range(per):
                    x_ref[k * per + p, s * CAP : (s + 1) * CAP, :] = in_ref[s * held + k, :, p * chunk : (p + 1) * chunk]
        acc_g[...] = jnp.zeros_like(acc_g)
        acc_u[...] = jnp.zeros_like(acc_u)

    x = x_ref[step]
    acc_g[...] += nn(x, gate_ref[0])
    acc_u[...] += nn(x, up_ref[0])

    @pl.when(step == pl.num_programs(0) - 1)
    def _():
        parts = []
        for s in range(seqs):
            total = jnp.zeros((CAP, 1), F32)
            for k in range(held):
                tail = in_ref[s * held + k, :, width : width + LANES].astype(F32)
                total += tail[:, 0:1] + tail[:, 1:2]
            parts.append(total)
        squares = jnp.concatenate(parts, axis=0)
        inverse = lax.rsqrt(squares / (held * width) + EPS)
        gate = acc_g[...] * inverse
        up = acc_u[...] * inverse
        out_ref[...] = (gate * (1.0 / (1.0 + jnp.exp(-gate))) * up).astype(BF16)


def down_kernel(seqs, order_ref, h_ref, w_ref, out_ref, acc):
    step = pl.program_id(0)

    @pl.when(step == 0)
    def _():
        acc[...] = jnp.zeros_like(acc)

    acc[...] += nn(h_ref[0], w_ref[0])

    @pl.when(step == pl.num_programs(0) - 1)
    def _():
        for s in range(seqs):
            out_ref[s, :, :] = acc[s * CAP : (s + 1) * CAP, :].astype(BF16)


def gates_kernel(held, total_width, parts, *refs):
    stats_refs, (ids_ref, place_ref, hi_ref, lo_ref) = refs[:parts], refs[parts:]
    total = stats_refs[0][...]
    for ref in stats_refs[1:]:
        total = total + ref[...]
    experts = total.shape[0] - 8
    inverse = lax.rsqrt(total[experts : experts + 1, :] / total_width + EPS)
    logits = total[0:experts, :] * inverse
    probs = 1.0 / (1.0 + jnp.exp(-logits))
    expert = iota(probs.shape, 0)
    ids = ids_ref[...]
    chosen = [
        jnp.sum(jnp.where(expert == ids[i : i + 1, :], probs, 0.0), axis=0, keepdims=True) for i in range(ids.shape[0])
    ]
    norm = chosen[0]
    for c in chosen[1:]:
        norm = norm + c
    for e in range(held):
        gate = jnp.zeros_like(norm)
        for i, c in enumerate(chosen):
            gate += jnp.where(ids[i : i + 1, :] == e, c / norm, 0.0)
        hi, lo = split_hi_lo(place_ref[e * CAP : (e + 1) * CAP, :] * gate)
        hi_ref[e * CAP : (e + 1) * CAP, :] = hi.astype(F32)
        lo_ref[e * CAP : (e + 1) * CAP, :] = lo.astype(F32)


def combine_kernel(held, mixed_ref, hi_ref, lo_ref, *refs):
    y_refs, out_ref = refs[:-1], refs[-1]
    if len(y_refs) > 1:
        y = jnp.concatenate([r[...].astype(F32) for r in y_refs], axis=0).astype(BF16)
    else:
        y = jnp.concatenate([y_refs[0][e].astype(F32) for e in range(held)], axis=0).astype(BF16)
    extra = tn(hi_ref[...].astype(BF16), y) + tn(lo_ref[...].astype(BF16), y)
    out_ref[...] = (mixed_ref[...].astype(F32) + extra).astype(BF16)


def call(body, out_shape, args, scratch=(), flops=0, nbytes=0):
    return pl.pallas_call(
        body,
        out_shape=out_shape,
        in_specs=[VMEM] * len(args),
        out_specs=jax.tree.map(lambda _: VMEM, out_shape),
        scratch_shapes=list(scratch),
        cost_estimate=pl.CostEstimate(flops=flops or 1000, bytes_accessed=nbytes or 1000, transcendentals=0),
    )(*args)


def shaped(shape, dtype):
    return jax.ShapeDtypeStruct(shape, dtype)


def general_body(
    residual, query_rows, key_rows, value_rows, log_decay, attn_gain, norm_gain, router, expert_ids, priority,
    gate_weight, up_weight, down_weight,
):
    rows, width = residual.shape
    heads = width // HEAD
    held = lax.axis_size("exp")
    seqs = lax.axis_size("seq")
    experts = router.shape[1]
    share_rows = width // seqs
    hidden_part = gate_weight.shape[2]
    out_part = down_weight.shape[2]
    ids = expert_ids.T
    payload, cum_row, cum_col = call(
        functools.partial(state_kernel, heads, seqs, share_rows),
        (
            shaped((seqs, share_rows + PAD, LANES), BF16),
            shaped((LANES, rows), F32),
            shaped((rows, LANES), F32),
        ),
        (key_rows, value_rows, log_decay.T),
        scratch=[pltpu.VMEM((LANES, rows), F32)],
        flops=60_000_000,
        nbytes=1_200_000,
    )
    arrived = lax.all_to_all(payload, "seq", split_axis=0, concat_axis=0, tiled=True)
    local = call(
        functools.partial(local_kernel, heads),
        shaped((rows, width), F32),
        (query_rows, key_rows, value_rows, cum_row, cum_col),
        flops=200_000_000,
        nbytes=2_000_000,
    )
    place = call(functools.partial(place_kernel, held), shaped((held * CAP, rows), F32), (ids, priority))
    prefix = call(functools.partial(scan_kernel, seqs, share_rows), shaped((seqs, share_rows, LANES), BF16), (arrived,))
    carried = lax.all_to_all(prefix, "seq", split_axis=0, concat_axis=0, tiled=True).reshape(width, LANES)
    mixed, slots, stats = call(
        functools.partial(mix_kernel, heads, held, seqs),
        (
            shaped((rows, width), BF16),
            shaped((seqs, held, CAP, width + LANES), BF16),
            shaped((experts + 8, rows), F32),
        ),
        (
            query_rows, local, carried, cum_col, residual, attn_gain[None], norm_gain[None], router.T, place,
        ),
        flops=200_000_000,
        nbytes=3_000_000,
    )
    slots = slots.reshape(seqs * held, CAP, width + LANES)
    gathered = lax.all_to_all(slots, ("seq", "exp"), split_axis=0, concat_axis=0, tiled=True)
    stat_parts = [stats]
    for r in range(1, held):
        stat_parts.append(lax.ppermute(stats, "exp", [(i, (i + r) % held) for i in range(held)]))
    slot_rows = seqs * CAP
    chunk = width // 2
    hidden = pl.pallas_call(
        functools.partial(gate_up_kernel, seqs, held, width, chunk),
        out_shape=shaped((slot_rows, hidden_part), BF16),
        grid=(held * width // chunk,),
        in_specs=[
            VMEM,
            pl.BlockSpec((1, chunk, hidden_part), lambda i: (0, i, 0)),
            pl.BlockSpec((1, chunk, hidden_part), lambda i: (0, i, 0)),
        ],
        out_specs=pl.BlockSpec((slot_rows, hidden_part), lambda i: (0, 0)),
        scratch_shapes=[
            pltpu.VMEM((held * width // chunk, slot_rows, chunk), BF16),
            pltpu.VMEM((slot_rows, hidden_part), F32),
            pltpu.VMEM((slot_rows, hidden_part), F32),
        ],
        name="gate_up",
        cost_estimate=pl.CostEstimate(flops=900_000_000, bytes_accessed=28_000_000, transcendentals=0),
    )(gathered, gate_weight, up_weight)
    me = lax.axis_index("seq")
    if seqs <= 8:
        parts = [hidden]
        for r in range(1, seqs):
            parts.append(lax.ppermute(hidden, "seq", [(i, (i + r) % seqs) for i in range(seqs)]))
        whole = jnp.stack(parts)
        order = jnp.mod(me - jnp.arange(seqs, dtype=jnp.int32), seqs)
    else:
        whole = lax.all_gather(hidden, "seq", axis=0)
        order = jnp.arange(seqs, dtype=jnp.int32)
    expert_out = pl.pallas_call(
        functools.partial(down_kernel, seqs),
        out_shape=shaped((seqs, CAP, out_part), BF16),
        grid_spec=pltpu.PrefetchScalarGridSpec(
            num_scalar_prefetch=1,
            grid=(seqs,),
            in_specs=[
                pl.BlockSpec((1, slot_rows, hidden_part), lambda i, o: (i, 0, 0)),
                pl.BlockSpec((1, hidden_part, out_part), lambda i, o: (0, o[i], 0)),
            ],
            out_specs=pl.BlockSpec((seqs, CAP, out_part), lambda i, o: (0, 0, 0)),
            scratch_shapes=[pltpu.VMEM((slot_rows, out_part), F32)],
        ),
        name="down",
        cost_estimate=pl.CostEstimate(flops=450_000_000, bytes_accessed=14_000_000, transcendentals=0),
    )(order, whole, down_weight)
    if seqs == held:
        pieces = []
        for r in range(seqs):
            target = [
                (s * held + e, ((e + r) % seqs) * held + s) for s in range(seqs) for e in range(held)
            ]
            mine = lax.dynamic_index_in_dim(
                expert_out, jnp.mod(lax.axis_index("exp") + r, seqs), axis=0, keepdims=False
            )
            pieces.append(lax.ppermute(mine, ("seq", "exp"), target))
        stacked = jnp.stack(pieces)
        source = jnp.mod(me - jnp.arange(held, dtype=jnp.int32), held)
        y = (jnp.take(stacked, source, axis=0),)
    else:
        returned = lax.all_to_all(expert_out, "seq", split_axis=0, concat_axis=1, tiled=True)
        returned = returned.reshape(CAP, seqs * out_part)
        y = (lax.all_to_all(returned[None], "exp", split_axis=2, concat_axis=0, tiled=True),)
    hi, lo = call(
        functools.partial(gates_kernel, held, held * width, len(stat_parts)),
        (shaped((held * CAP, rows), F32),) * 2,
        (*stat_parts, ids, place),
    )
    return call(functools.partial(combine_kernel, held), shaped((rows, width), BF16), (mixed, hi, lo, *y))


def state_pieces_kernel(heads, seqs, k_ref, v_ref, decay_ref, *refs):
    pieces, row_ref, col_ref, pad_ref, end_ref = refs[:seqs], *refs[seqs:]
    rows = k_ref.shape[0]
    per = heads // seqs
    me = lax.axis_index("seq")
    pad_ref[...] = jnp.zeros_like(pad_ref)
    pad_ref[0:heads, :] = decay_ref[...]
    log_decay = pad_ref[...]
    lower = jnp.where(iota((rows, rows), 0) >= iota((rows, rows), 1), 1.0, 0.0).astype(F32)
    cum_col = lax.dot_general(
        lower, log_decay, (((1,), (1,)), ((), ())), precision=lax.Precision.HIGHEST, preferred_element_type=F32
    )
    cum_row = lax.dot_general(
        log_decay, lower, (((1,), (1,)), ((), ())), precision=lax.Precision.HIGHEST, preferred_element_type=F32
    )
    row_ref[...] = cum_row
    col_ref[...] = cum_col
    end_ref[...] = jnp.exp(cum_row[:, rows - 1 : rows] - cum_row)
    hi, lo = split_hi_lo(jnp.exp(cum_col[rows - 1 : rows, :]))
    tail = jnp.concatenate([jnp.broadcast_to(hi, (8, LANES)), jnp.broadcast_to(lo, (8, LANES))], axis=0)
    for r in range(seqs):
        share = lax.rem(me + r, seqs)
        for j in range(per):
            h = share * per + j
            cols = pl.ds(pl.multiple_of(h * HEAD, HEAD), HEAD)
            keyed = (k_ref[:, cols].astype(F32).T * end_ref[pl.ds(h, 1), :]).astype(BF16)
            pieces[r][j * HEAD : (j + 1) * HEAD, :] = nn(keyed, v_ref[:, cols]).astype(BF16)
        pieces[r][per * HEAD : per * HEAD + PAD, :] = tail


def pack_kernel(heads, router_ref, gain_ref, out_ref):
    experts = router_ref.shape[0]
    out_ref[0:experts, :] = router_ref[...]
    hi, lo = split_hi_lo(gain_ref[...])
    hi, lo = hi.astype(F32), lo.astype(F32)
    at = iota((PAD, HEAD), 0)
    for h in range(heads):
        both = jnp.where(at == 0, hi[h : h + 1, :], jnp.where(at == 1, lo[h : h + 1, :], 0.0))
        out_ref[experts : experts + PAD, h * HEAD : (h + 1) * HEAD] = both.astype(BF16)


def rows_kernel(
    heads, seqs, held, q_ref, k_ref, v_ref, res_ref, row_ref, col_ref, ids_ref, prio_ref, local_ref, grown_ref,
    place_ref, *pieces,
):
    place_kernel(held, ids_ref, prio_ref, place_ref)
    rows = q_ref.shape[0]
    causal = iota((rows, rows), 0) >= iota((rows, rows), 1)
    grow = jnp.exp(col_ref[...])
    for h in range(heads):
        cols = slice(h * HEAD, (h + 1) * HEAD)
        q = q_ref[:, cols]
        scores = nt(q, k_ref[:, cols])
        spread = col_ref[:, h : h + 1] - row_ref[h : h + 1, :]
        near = jnp.where(causal, scores * jnp.exp(jnp.where(causal, spread, 0.0)), 0.0).astype(BF16)
        local_ref[:, cols] = nn(near, v_ref[:, cols])
        grown_ref[:, cols] = (q.astype(F32) * grow[:, h : h + 1]).astype(BF16)
    place = place_ref[...]
    ids = ids_ref[...].astype(F32)
    lane = iota((held * CAP, LANES), 1)
    extra = jnp.zeros((held * CAP, LANES), F32)
    for i in range(ids.shape[0]):
        extra = jnp.where(lane == i, jnp.sum(place * ids[i : i + 1, :], axis=1, keepdims=True), extra)
    place = place.astype(BF16)
    me = lax.axis_index("seq")
    part = heads * HEAD // seqs
    for r in range(seqs):
        cols = pl.ds(pl.multiple_of(lax.rem(me + r, seqs) * part, part), part)
        pieces[r][:, 0:part] = nn(place, grown_ref[:, cols]).astype(BF16)
        pieces[r][:, part : 2 * part] = nn(place, local_ref[:, cols].astype(BF16)).astype(BF16)
        pieces[r][:, 2 * part : 3 * part] = nn(place, res_ref[:, cols]).astype(BF16)
        pieces[r][:, 3 * part : 3 * part + LANES] = extra.astype(BF16)


def keep_kernel(count, *refs):
    sources, kept, sems = refs[1 : count + 1], refs[count + 1 : 2 * count + 1], refs[2 * count + 1]
    copies = [pltpu.make_async_copy(w, b, sems.at[i]) for i, (w, b) in enumerate(zip(sources, kept))]
    for copy in copies:
        copy.start()
    for copy in copies:
        copy.wait()


def owner_kernel(heads, seqs, held, again_ref, *refs):
    states, rows_in = refs[:seqs], refs[seqs : 2 * seqs]
    slots_ref, ids_ref, *rest = refs[2 * seqs :]
    prefixes, (state_ref, rows_ref, prefix_ref) = rest[:seqs], rest[seqs:]
    per = heads // seqs
    part = per * HEAD
    me = lax.axis_index("seq")
    expert = lax.axis_index("exp")
    for r in range(seqs):
        b = lax.rem(me + seqs - r, seqs)
        state_ref[b] = states[r][...]
        rows_ref[b] = rows_in[r][...]
        mine = rows_in[r][:, 3 * part : 3 * part + LANES].astype(F32)
        picked = jnp.zeros((CAP, LANES), F32)
        for e in range(held):
            picked = jnp.where(expert == e, mine[e * CAP : (e + 1) * CAP, :], picked)
        ids_ref[pl.ds(pl.multiple_of(b * CAP, CAP), CAP), :] = picked
    lane = iota((1, LANES), 1)
    for j in range(per):
        h = me * per + j
        again = again_ref[pl.ds(h, 1), :]
        cols = slice(j * HEAD, (j + 1) * HEAD)
        carry = jnp.zeros((HEAD, HEAD), F32)
        for b in range(seqs):
            prefix = carry.astype(BF16)
            prefix_ref[b, cols, :] = prefix
            attended = rows_ref[b, :, part + j * HEAD : part + (j + 1) * HEAD].astype(F32)
            if b > 0:
                attended = attended + nn(rows_ref[b, :, cols], prefix)
            power = jnp.mean(attended * attended, axis=1, keepdims=True)
            normed = attended * lax.rsqrt(power + EPS) * again
            residual = rows_ref[b, :, 2 * part + j * HEAD : 2 * part + (j + 1) * HEAD].astype(F32)
            mixed = (residual + normed).astype(BF16)
            for e in range(held):
                piece = mixed[e * CAP : (e + 1) * CAP, :]
                for s in range(seqs):
                    slots_ref[s, e, b * CAP : (b + 1) * CAP, cols] = piece
            if b + 1 < seqs:
                tail = state_ref[b, part : part + PAD, :].astype(F32)
                decay = jnp.where(lane == h, tail[0:1, :] + tail[8:9, :], 0.0)
                carry = jnp.sum(decay, axis=1, keepdims=True) * carry + state_ref[b, cols, :].astype(F32)
    for r in range(seqs):
        prefixes[r][...] = prefix_ref[lax.rem(me + r, seqs)]


def expert_in_kernel(seqs, held, width, in_ref, ids_ref, gate_ref, up_ref, *refs):
    tables, (out_ref, share_ref, x_ref) = refs[:held], refs[held:]
    part = in_ref.shape[2]
    slot_rows = in_ref.shape[1]
    experts = tables[0].shape[0] - PAD
    expert = lax.axis_index("exp")
    squares = jnp.zeros((slot_rows, 1), F32)
    for i in range(seqs * held):
        piece = in_ref[i].astype(F32)
        squares += jnp.sum(piece * piece, axis=1, keepdims=True)
    inverse = lax.rsqrt(squares / (held * width) + EPS)
    logits = jnp.zeros((slot_rows, experts), F32)
    for r in range(held):
        k = lax.rem(expert + held - r, held)
        for s in range(seqs):
            cols = slice(s * part, (s + 1) * part)
            gain = tables[r][experts : experts + PAD, cols].astype(F32)
            gain = gain[0:1, :] + gain[1:2, :]
            scaled = in_ref[s * held + k].astype(F32) * gain * inverse
            hi, lo = split_hi_lo(scaled)
            x_ref[:, pl.ds(pl.multiple_of(k * width + s * part, part), part)] = hi
            logits += nt(hi, tables[r][0:experts, cols]) + nt(lo, tables[r][0:experts, cols])
    probs = 1.0 / (1.0 + jnp.exp(-logits))
    lane = iota(probs.shape, 1)
    total = jnp.zeros((slot_rows, 1), F32)
    for i in range(2):
        number = ids_ref[:, i : i + 1].astype(jnp.int32)
        total += jnp.sum(jnp.where(lane == number, probs, 0.0), axis=1, keepdims=True)
    own = jnp.sum(jnp.where(lane == expert, probs, 0.0), axis=1, keepdims=True)
    share_ref[...] = jnp.broadcast_to(own / total, share_ref.shape)
    x = x_ref[...]
    gate = nn(x, gate_ref[0])
    up = nn(x, up_ref[0])
    out_ref[...] = (gate * (1.0 / (1.0 + jnp.exp(-gate))) * up).astype(BF16)


def expert_out_kernel(seqs, held, w_ref, share_ref, *refs):
    h_refs, out_refs, acc_ref = refs[:seqs], refs[seqs : seqs + held], refs[seqs + held]
    part = h_refs[0].shape[-1]
    me, expert = lax.axis_index("seq"), lax.axis_index("exp")
    total = None
    for r in range(seqs):
        at = pl.multiple_of(lax.rem(me + seqs - r, seqs) * part, part)
        term = nn(h_refs[r][...], w_ref[0, pl.ds(at, part), :])
        total = term if total is None else total + term
    acc_ref[...] = total * share_ref[:, 0:1]
    for r in range(held):
        at = pl.multiple_of(lax.rem(expert + r, seqs) * CAP, CAP)
        out_refs[r][...] = acc_ref[pl.ds(at, CAP), :].astype(BF16)


def mixed_kernel(heads, seqs, grown_ref, local_ref, res_ref, again_ref, *refs):
    prefixes, mixed_ref = refs[:seqs], refs[seqs]
    me = lax.axis_index("seq")
    per = heads // seqs
    for r in range(seqs):
        share = lax.rem(me + seqs - r, seqs)
        for j in range(per):
            h = share * per + j
            cols = pl.ds(pl.multiple_of(h * HEAD, HEAD), HEAD)
            inter = nn(grown_ref[:, cols], prefixes[r][j * HEAD : (j + 1) * HEAD, :])
            attended = local_ref[:, cols] + inter
            power = jnp.mean(attended * attended, axis=1, keepdims=True)
            normed = attended * lax.rsqrt(power + EPS) * again_ref[pl.ds(h, 1), :]
            mixed_ref[:, cols] = (res_ref[:, cols].astype(F32) + normed).astype(BF16)


def add_kernel(held, mixed_ref, place_ref, *refs):
    y_refs, out_ref, y_ref = refs[:held], refs[held], refs[held + 1]
    me = lax.axis_index("seq")
    for r, ref in enumerate(y_refs):
        at = pl.multiple_of(lax.rem(me + held - r, held) * CAP, CAP)
        y_ref[pl.ds(at, CAP), :] = ref[...].astype(F32)
    extra = tn(place_ref[...].astype(BF16), y_ref[...].astype(BF16))
    out_ref[...] = (mixed_ref[...].astype(F32) + extra).astype(BF16)


def run(body, out_shape, args, scratch=(), flops=1000, nbytes=1000, vmem=SMALL, anywhere=0):
    outs = out_shape if isinstance(out_shape, tuple) else (out_shape,)
    specs = tuple(VMEM for _ in outs)
    return pl.pallas_call(
        body,
        out_shape=out_shape,
        in_specs=[VMEM] * (len(args) - anywhere) + [pl.BlockSpec(memory_space=pltpu.HBM)] * anywhere,
        out_specs=specs if isinstance(out_shape, tuple) else specs[0],
        scratch_shapes=list(scratch),
        compiler_params=pltpu.CompilerParams(vmem_limit_bytes=vmem),
        cost_estimate=pl.CostEstimate(flops=flops, bytes_accessed=nbytes, transcendentals=0),
    )(*args)


def keep(weights, after):
    return run(
        functools.partial(keep_kernel, len(weights)),
        tuple(pltpu.VMEM(w.shape, w.dtype) for w in weights),
        (after, *(pltpu.with_memory_space_constraint(w, pltpu.HBM) for w in weights)),
        scratch=[pltpu.SemaphoreType.DMA((len(weights),))],
        nbytes=sum(w.size * 2 for w in weights),
        anywhere=len(weights),
    )


def rotate(x, axis, count, step):
    return lax.ppermute(x, axis, [(i, (i + step) % count) for i in range(count)])


def spread(pieces, axis, count):
    return [pieces[0]] + [rotate(pieces[r], axis, count, r) for r in range(1, count)]


def ring_body(
    residual, query_rows, key_rows, value_rows, log_decay, attn_gain, norm_gain, router, expert_ids, priority,
    gate_weight, up_weight, down_weight,
):
    rows, width = residual.shape
    heads = width // HEAD
    held = lax.axis_size("exp")
    seqs = lax.axis_size("seq")
    experts = router.shape[1]
    part = width // seqs
    slot_rows = seqs * CAP
    hidden_part = gate_weight.shape[2]
    out_part = down_weight.shape[2]
    again = attn_gain.reshape(heads, HEAD)
    *pieces, cum_row, cum_col = run(
        functools.partial(state_pieces_kernel, heads, seqs),
        (
            *(shaped((part + PAD, LANES), BF16) for _ in range(seqs)),
            shaped((LANES, rows), F32),
            shaped((rows, LANES), F32),
        ),
        (key_rows, value_rows, log_decay.T),
        scratch=[pltpu.VMEM((LANES, rows), F32), pltpu.VMEM((LANES, rows), F32)],
    )
    states = spread(pieces, "seq", seqs)
    table = run(
        functools.partial(pack_kernel, heads),
        shaped((experts + PAD, width), BF16),
        (router.T, norm_gain.reshape(heads, HEAD)),
    )
    tables = spread([table] * held, "exp", held)
    local, grown, place, *row_pieces = run(
        functools.partial(rows_kernel, heads, seqs, held),
        (
            shaped((rows, width), F32),
            shaped((rows, width), BF16),
            shaped((held * CAP, rows), F32),
            *(shaped((held * CAP, 3 * part + LANES), BF16) for _ in range(seqs)),
        ),
        (query_rows, key_rows, value_rows, residual, cum_row, cum_col, expert_ids.T, priority),
        flops=200_000_000,
        nbytes=2_000_000,
    )
    row_parts = spread(row_pieces, "seq", seqs)
    weights = keep((gate_weight, up_weight), row_pieces[0])
    slots, slot_ids, *prefixes = run(
        functools.partial(owner_kernel, heads, seqs, held),
        (
            pltpu.VMEM((seqs, held, slot_rows, part), BF16),
            shaped((slot_rows, LANES), F32),
            *(shaped((part, LANES), BF16) for _ in range(seqs)),
        ),
        (again, *states, *row_parts),
        scratch=[
            pltpu.VMEM((seqs, part + PAD, LANES), BF16),
            pltpu.VMEM((seqs, held * CAP, 3 * part + LANES), BF16),
            pltpu.VMEM((seqs, part, LANES), BF16),
        ],
    )
    slots = slots.reshape(seqs * held, slot_rows, part)
    gathered = lax.all_to_all(slots, ("seq", "exp"), split_axis=0, concat_axis=0, tiled=True)
    hidden, shares = run(
        functools.partial(expert_in_kernel, seqs, held, width),
        (shaped((slot_rows, hidden_part), BF16), shaped((slot_rows, LANES), F32)),
        (gathered, slot_ids, weights[0], weights[1], *tables),
        scratch=[pltpu.VMEM((slot_rows, held * width), BF16)],
        flops=900_000_000,
        nbytes=28_000_000,
    )
    hiddens = spread([hidden] * seqs, "seq", seqs)
    prefixes, hidden = lax.optimization_barrier((prefixes, hidden))
    returned = spread(prefixes, "seq", seqs)
    (down_weight,) = keep((down_weight,), hidden)
    outs = run(
        functools.partial(expert_out_kernel, seqs, held),
        (shaped((CAP, out_part), BF16),) * held,
        (down_weight, shares, *hiddens),
        scratch=[pltpu.VMEM((slot_rows, out_part), F32)],
        flops=450_000_000,
        nbytes=14_000_000,
    )
    y = [
        lax.ppermute(
            piece,
            ("seq", "exp"),
            [(s * held + e, ((e + r) % seqs) * held + s) for s in range(seqs) for e in range(held)],
        )
        for r, piece in enumerate(outs)
    ]
    mixed = run(
        functools.partial(mixed_kernel, heads, seqs),
        shaped((rows, width), BF16),
        (grown, local, residual, again, *returned),
        flops=100_000_000,
        nbytes=2_000_000,
    )
    return run(
        functools.partial(add_kernel, held),
        shaped((rows, width), BF16),
        (mixed, place, *y),
        scratch=[pltpu.VMEM((held * CAP, width), F32)],
    )


def body(residual, *args):
    seqs, held = lax.axis_size("seq"), lax.axis_size("exp")
    if seqs == held and (residual.shape[1] // HEAD) % seqs == 0:
        return ring_body(residual, *args)
    return general_body(residual, *args)


def solution(mesh):
    token = P(("groups", "seq"), "exp")
    return jax.shard_map(
        body,
        mesh=mesh,
        in_specs=(
            token, token, token, token, token, P("exp"), P("exp"), P("exp", None),
            P(("groups", "seq"), None), P(("groups", "seq"), None),
            P("exp", None, "seq"), P("exp", None, "seq"), P("exp", None, "seq"),
        ),
        out_specs=token,
        check_vma=False,
    )
```

```python
import functools

import jax
import jax.numpy as jnp
from jax import lax
from jax.experimental import pallas as pl
from jax.experimental.pallas import tpu as pltpu
from jax.sharding import PartitionSpec as P


HEAD = 128
LANES = 128
CAP = 8
PAD = 16
EPS = 1e-06
SMALL = 8 << 20
F32 = jnp.float32
BF16 = jnp.bfloat16


VMEM = pl.BlockSpec(memory_space=pltpu.VMEM)


def nt(a, b):
    return lax.dot_general(a, b, (((1,), (1,)), ((), ())), preferred_element_type=F32)


def tn(a, b):
    return lax.dot_general(a, b, (((0,), (0,)), ((), ())), preferred_element_type=F32)


def nn(a, b):
    return lax.dot_general(a, b, (((1,), (0,)), ((), ())), preferred_element_type=F32)


def iota(shape, dim):
    return lax.broadcasted_iota(jnp.int32, shape, dim)


def split_hi_lo(x):
    hi = x.astype(BF16)
    return hi, (x - hi.astype(F32)).astype(BF16)


def state_kernel(heads, shares, share_rows, k_ref, v_ref, decay_ref, pay_ref, row_ref, col_ref, pad_ref):
    rows = k_ref.shape[0]
    pad_ref[...] = jnp.zeros_like(pad_ref)
    pad_ref[0:heads, :] = decay_ref[...]
    log_decay = pad_ref[...]
    lower = jnp.where(iota((rows, rows), 0) >= iota((rows, rows), 1), 1.0, 0.0).astype(F32)
    cum_col = lax.dot_general(
        lower, log_decay, (((1,), (1,)), ((), ())), precision=lax.Precision.HIGHEST, preferred_element_type=F32
    )
    cum_row = lax.dot_general(
        log_decay, lower, (((1,), (1,)), ((), ())), precision=lax.Precision.HIGHEST, preferred_element_type=F32
    )
    row_ref[...] = cum_row
    col_ref[...] = cum_col
    to_end = jnp.exp(cum_col[rows - 1 : rows, :] - cum_col)
    hi, lo = split_hi_lo(jnp.exp(cum_col[rows - 1 : rows, :]))
    for s in range(shares):
        pay_ref[s, share_rows : share_rows + PAD, :] = jnp.concatenate(
            [jnp.broadcast_to(hi, (8, LANES)), jnp.broadcast_to(lo, (8, LANES))], axis=0
        )
    for h in range(heads):
        cols = slice(h * HEAD, (h + 1) * HEAD)
        keyed = (k_ref[:, cols].astype(F32) * to_end[:, h : h + 1]).astype(BF16)
        state = tn(keyed, v_ref[:, cols]).astype(BF16)
        at = h * HEAD
        while at < (h + 1) * HEAD:
            share, inner = divmod(at, share_rows)
            take = min(share_rows - inner, (h + 1) * HEAD - at)
            pay_ref[share, inner : inner + take, :] = state[at - h * HEAD : at - h * HEAD + take, :]
            at += take


def local_kernel(heads, q_ref, k_ref, v_ref, row_ref, col_ref, out_ref):
    rows = q_ref.shape[0]
    causal = iota((rows, rows), 0) >= iota((rows, rows), 1)
    for h in range(heads):
        cols = slice(h * HEAD, (h + 1) * HEAD)
        scores = nt(q_ref[:, cols], k_ref[:, cols])
        spread = col_ref[:, h : h + 1] - row_ref[h : h + 1, :]
        weights = jnp.where(causal, scores * jnp.exp(jnp.where(causal, spread, 0.0)), 0.0).astype(BF16)
        out_ref[:, cols] = nn(weights, v_ref[:, cols])


def place_kernel(held, ids_ref, prio_ref, place_ref):
    rows = ids_ref.shape[1]
    order = prio_ref[...].astype(F32)
    across = jnp.broadcast_to(order, (rows, rows))
    earlier = jnp.where(across.T < across, 1.0, 0.0).astype(BF16)
    ids = ids_ref[...]
    expert = iota((8 * pl.cdiv(held, 8), rows), 0)
    hit = expert == ids[0:1, :]
    for i in range(1, ids.shape[0]):
        hit = hit | (expert == ids[i : i + 1, :])
    member = jnp.where(hit, 1.0, 0.0)
    rank = nn(member.astype(BF16), earlier)
    slot = iota((CAP, rows), 0).astype(F32)
    for e in range(held):
        chosen = (member[e : e + 1, :] > 0.5) & (rank[e : e + 1, :] == slot)
        place_ref[e * CAP : (e + 1) * CAP, :] = jnp.where(chosen, 1.0, 0.0)


def scan_kernel(shares, share_rows, in_ref, out_ref):
    me = lax.axis_index("seq")
    row = me * share_rows + iota((share_rows, LANES), 0)
    onehot = jnp.where(row // HEAD == iota((share_rows, LANES), 1), 1.0, 0.0)
    carry = jnp.zeros((share_rows, LANES), F32)
    for b in range(shares):
        out_ref[b, :, :] = carry.astype(BF16)
        if b + 1 < shares:
            tail = in_ref[b, share_rows : share_rows + PAD, :].astype(F32)
            decay = tail[0:1, :] + tail[8:9, :]
            each = jnp.sum(onehot * decay, axis=1, keepdims=True)
            carry = each * carry + in_ref[b, 0:share_rows, :].astype(F32)


def mix_kernel(
    heads, held, copies, q_ref, local_ref, carried_ref, col_ref, res_ref, again_ref, ngain_ref, router_ref, place_ref,
    mixed_ref, slots_ref, stats_ref,
):
    rows = q_ref.shape[0]
    width = heads * HEAD
    experts = router_ref.shape[0]
    place = place_ref[...].astype(BF16)
    grow = jnp.exp(col_ref[...])
    squares = jnp.zeros((rows, 1), F32)
    picked_squares = jnp.zeros((held * CAP, 1), F32)
    logits = jnp.zeros((experts, rows), F32)
    for h in range(heads):
        cols = slice(h * HEAD, (h + 1) * HEAD)
        inter = nn(q_ref[:, cols], carried_ref[h * HEAD : (h + 1) * HEAD, :])
        attended = local_ref[:, cols] + grow[:, h : h + 1] * inter
        power = jnp.mean(attended * attended, axis=1, keepdims=True)
        normed = attended * lax.rsqrt(power + EPS) * again_ref[:, cols]
        mixed = (res_ref[:, cols].astype(F32) + normed).astype(BF16)
        mixed_ref[:, cols] = mixed
        mixed_f = mixed.astype(F32)
        squares += jnp.sum(mixed_f * mixed_f, axis=1, keepdims=True)
        hi, lo = split_hi_lo(mixed_f * ngain_ref[:, cols])
        logits += nt(router_ref[:, cols], hi) + nt(router_ref[:, cols], lo)
        picked = nn(place, mixed)
        picked_squares += jnp.sum(picked * picked, axis=1, keepdims=True)
        sent = (picked * ngain_ref[:, cols]).astype(BF16)
        for s in range(copies):
            for e in range(held):
                slots_ref[s, e, :, cols] = sent[e * CAP : (e + 1) * CAP, :]
    lane = iota((held * CAP, LANES), 1)
    hi, lo = split_hi_lo(picked_squares)
    extra = jnp.where(lane == 0, hi.astype(F32), jnp.where(lane == 1, lo.astype(F32), 0.0)).astype(BF16)
    for s in range(copies):
        for e in range(held):
            slots_ref[s, e, :, width : width + LANES] = extra[e * CAP : (e + 1) * CAP, :]
    stats_ref[0:experts, :] = logits
    stats_ref[experts : experts + 8, :] = jnp.broadcast_to(squares, (rows, rows)).T[0:8, :]


def gate_up_kernel(seqs, held, width, chunk, in_ref, gate_ref, up_ref, out_ref, x_ref, acc_g, acc_u):
    step = pl.program_id(0)
    per = width // chunk

    @pl.when(step == 0)
    def _():
        for s in range(seqs):
            for k in range(held):
                for p in range(per):
                    x_ref[k * per + p, s * CAP : (s + 1) * CAP, :] = in_ref[s * held + k, :, p * chunk : (p + 1) * chunk]
        acc_g[...] = jnp.zeros_like(acc_g)
        acc_u[...] = jnp.zeros_like(acc_u)

    x = x_ref[step]
    acc_g[...] += nn(x, gate_ref[0])
    acc_u[...] += nn(x, up_ref[0])

    @pl.when(step == pl.num_programs(0) - 1)
    def _():
        parts = []
        for s in range(seqs):
            total = jnp.zeros((CAP, 1), F32)
            for k in range(held):
                tail = in_ref[s * held + k, :, width : width + LANES].astype(F32)
                total += tail[:, 0:1] + tail[:, 1:2]
            parts.append(total)
        squares = jnp.concatenate(parts, axis=0)
        inverse = lax.rsqrt(squares / (held * width) + EPS)
        gate = acc_g[...] * inverse
        up = acc_u[...] * inverse
        out_ref[...] = (gate * (1.0 / (1.0 + jnp.exp(-gate))) * up).astype(BF16)


def down_kernel(seqs, order_ref, h_ref, w_ref, out_ref, acc):
    step = pl.program_id(0)

    @pl.when(step == 0)
    def _():
        acc[...] = jnp.zeros_like(acc)

    acc[...] += nn(h_ref[0], w_ref[0])

    @pl.when(step == pl.num_programs(0) - 1)
    def _():
        for s in range(seqs):
            out_ref[s, :, :] = acc[s * CAP : (s + 1) * CAP, :].astype(BF16)


def gates_kernel(held, total_width, parts, *refs):
    stats_refs, (ids_ref, place_ref, hi_ref, lo_ref) = refs[:parts], refs[parts:]
    total = stats_refs[0][...]
    for ref in stats_refs[1:]:
        total = total + ref[...]
    experts = total.shape[0] - 8
    inverse = lax.rsqrt(total[experts : experts + 1, :] / total_width + EPS)
    logits = total[0:experts, :] * inverse
    probs = 1.0 / (1.0 + jnp.exp(-logits))
    expert = iota(probs.shape, 0)
    ids = ids_ref[...]
    chosen = [
        jnp.sum(jnp.where(expert == ids[i : i + 1, :], probs, 0.0), axis=0, keepdims=True) for i in range(ids.shape[0])
    ]
    norm = chosen[0]
    for c in chosen[1:]:
        norm = norm + c
    for e in range(held):
        gate = jnp.zeros_like(norm)
        for i, c in enumerate(chosen):
            gate += jnp.where(ids[i : i + 1, :] == e, c / norm, 0.0)
        hi, lo = split_hi_lo(place_ref[e * CAP : (e + 1) * CAP, :] * gate)
        hi_ref[e * CAP : (e + 1) * CAP, :] = hi.astype(F32)
        lo_ref[e * CAP : (e + 1) * CAP, :] = lo.astype(F32)


def combine_kernel(held, mixed_ref, hi_ref, lo_ref, *refs):
    y_refs, out_ref = refs[:-1], refs[-1]
    if len(y_refs) > 1:
        y = jnp.concatenate([r[...].astype(F32) for r in y_refs], axis=0).astype(BF16)
    else:
        y = jnp.concatenate([y_refs[0][e].astype(F32) for e in range(held)], axis=0).astype(BF16)
    extra = tn(hi_ref[...].astype(BF16), y) + tn(lo_ref[...].astype(BF16), y)
    out_ref[...] = (mixed_ref[...].astype(F32) + extra).astype(BF16)


def call(body, out_shape, args, scratch=(), flops=0, nbytes=0):
    return pl.pallas_call(
        body,
        out_shape=out_shape,
        in_specs=[VMEM] * len(args),
        out_specs=jax.tree.map(lambda _: VMEM, out_shape),
        scratch_shapes=list(scratch),
        cost_estimate=pl.CostEstimate(flops=flops or 1000, bytes_accessed=nbytes or 1000, transcendentals=0),
    )(*args)


def shaped(shape, dtype):
    return jax.ShapeDtypeStruct(shape, dtype)


def general_body(
    residual, query_rows, key_rows, value_rows, log_decay, attn_gain, norm_gain, router, expert_ids, priority,
    gate_weight, up_weight, down_weight,
):
    rows, width = residual.shape
    heads = width // HEAD
    held = lax.axis_size("exp")
    seqs = lax.axis_size("seq")
    experts = router.shape[1]
    share_rows = width // seqs
    hidden_part = gate_weight.shape[2]
    out_part = down_weight.shape[2]
    ids = expert_ids.T
    payload, cum_row, cum_col = call(
        functools.partial(state_kernel, heads, seqs, share_rows),
        (
            shaped((seqs, share_rows + PAD, LANES), BF16),
            shaped((LANES, rows), F32),
            shaped((rows, LANES), F32),
        ),
        (key_rows, value_rows, log_decay.T),
        scratch=[pltpu.VMEM((LANES, rows), F32)],
        flops=60_000_000,
        nbytes=1_200_000,
    )
    arrived = lax.all_to_all(payload, "seq", split_axis=0, concat_axis=0, tiled=True)
    local = call(
        functools.partial(local_kernel, heads),
        shaped((rows, width), F32),
        (query_rows, key_rows, value_rows, cum_row, cum_col),
        flops=200_000_000,
        nbytes=2_000_000,
    )
    place = call(functools.partial(place_kernel, held), shaped((held * CAP, rows), F32), (ids, priority))
    prefix = call(functools.partial(scan_kernel, seqs, share_rows), shaped((seqs, share_rows, LANES), BF16), (arrived,))
    carried = lax.all_to_all(prefix, "seq", split_axis=0, concat_axis=0, tiled=True).reshape(width, LANES)
    mixed, slots, stats = call(
        functools.partial(mix_kernel, heads, held, seqs),
        (
            shaped((rows, width), BF16),
            shaped((seqs, held, CAP, width + LANES), BF16),
            shaped((experts + 8, rows), F32),
        ),
        (
            query_rows, local, carried, cum_col, residual, attn_gain[None], norm_gain[None], router.T, place,
        ),
        flops=200_000_000,
        nbytes=3_000_000,
    )
    slots = slots.reshape(seqs * held, CAP, width + LANES)
    gathered = lax.all_to_all(slots, ("seq", "exp"), split_axis=0, concat_axis=0, tiled=True)
    stat_parts = [stats]
    for r in range(1, held):
        stat_parts.append(lax.ppermute(stats, "exp", [(i, (i + r) % held) for i in range(held)]))
    slot_rows = seqs * CAP
    chunk = width // 2
    hidden = pl.pallas_call(
        functools.partial(gate_up_kernel, seqs, held, width, chunk),
        out_shape=shaped((slot_rows, hidden_part), BF16),
        grid=(held * width // chunk,),
        in_specs=[
            VMEM,
            pl.BlockSpec((1, chunk, hidden_part), lambda i: (0, i, 0)),
            pl.BlockSpec((1, chunk, hidden_part), lambda i: (0, i, 0)),
        ],
        out_specs=pl.BlockSpec((slot_rows, hidden_part), lambda i: (0, 0)),
        scratch_shapes=[
            pltpu.VMEM((held * width // chunk, slot_rows, chunk), BF16),
            pltpu.VMEM((slot_rows, hidden_part), F32),
            pltpu.VMEM((slot_rows, hidden_part), F32),
        ],
        name="gate_up",
        cost_estimate=pl.CostEstimate(flops=900_000_000, bytes_accessed=28_000_000, transcendentals=0),
    )(gathered, gate_weight, up_weight)
    me = lax.axis_index("seq")
    if seqs <= 8:
        parts = [hidden]
        for r in range(1, seqs):
            parts.append(lax.ppermute(hidden, "seq", [(i, (i + r) % seqs) for i in range(seqs)]))
        whole = jnp.stack(parts)
        order = jnp.mod(me - jnp.arange(seqs, dtype=jnp.int32), seqs)
    else:
        whole = lax.all_gather(hidden, "seq", axis=0)
        order = jnp.arange(seqs, dtype=jnp.int32)
    expert_out = pl.pallas_call(
        functools.partial(down_kernel, seqs),
        out_shape=shaped((seqs, CAP, out_part), BF16),
        grid_spec=pltpu.PrefetchScalarGridSpec(
            num_scalar_prefetch=1,
            grid=(seqs,),
            in_specs=[
                pl.BlockSpec((1, slot_rows, hidden_part), lambda i, o: (i, 0, 0)),
                pl.BlockSpec((1, hidden_part, out_part), lambda i, o: (0, o[i], 0)),
            ],
            out_specs=pl.BlockSpec((seqs, CAP, out_part), lambda i, o: (0, 0, 0)),
            scratch_shapes=[pltpu.VMEM((slot_rows, out_part), F32)],
        ),
        name="down",
        cost_estimate=pl.CostEstimate(flops=450_000_000, bytes_accessed=14_000_000, transcendentals=0),
    )(order, whole, down_weight)
    if seqs == held:
        pieces = []
        for r in range(seqs):
            target = [
                (s * held + e, ((e + r) % seqs) * held + s) for s in range(seqs) for e in range(held)
            ]
            mine = lax.dynamic_index_in_dim(
                expert_out, jnp.mod(lax.axis_index("exp") + r, seqs), axis=0, keepdims=False
            )
            pieces.append(lax.ppermute(mine, ("seq", "exp"), target))
        stacked = jnp.stack(pieces)
        source = jnp.mod(me - jnp.arange(held, dtype=jnp.int32), held)
        y = (jnp.take(stacked, source, axis=0),)
    else:
        returned = lax.all_to_all(expert_out, "seq", split_axis=0, concat_axis=1, tiled=True)
        returned = returned.reshape(CAP, seqs * out_part)
        y = (lax.all_to_all(returned[None], "exp", split_axis=2, concat_axis=0, tiled=True),)
    hi, lo = call(
        functools.partial(gates_kernel, held, held * width, len(stat_parts)),
        (shaped((held * CAP, rows), F32),) * 2,
        (*stat_parts, ids, place),
    )
    return call(functools.partial(combine_kernel, held), shaped((rows, width), BF16), (mixed, hi, lo, *y))


def state_pieces_kernel(heads, seqs, count, *refs):
    sources, kept, refs = refs[:count], refs[count : 2 * count], refs[2 * count :]
    pieces, row_ref, col_ref, pad_ref, end_ref, sems = refs[:seqs], *refs[seqs:]
    copies = [pltpu.make_async_copy(a, b, sems.at[i]) for i, (a, b) in enumerate(zip(sources, kept))]
    for copy in copies:
        copy.start()
    k_ref, v_ref, decay_ref = kept[:3]
    copies[2].wait()
    rows = k_ref.shape[0]
    per = heads // seqs
    me = lax.axis_index("seq")
    pad_ref[...] = jnp.zeros_like(pad_ref)
    pad_ref[0:heads, :] = decay_ref[...]
    log_decay = pad_ref[...]
    lower = jnp.where(iota((rows, rows), 0) >= iota((rows, rows), 1), 1.0, 0.0).astype(F32)
    cum_col = lax.dot_general(
        lower, log_decay, (((1,), (1,)), ((), ())), precision=lax.Precision.HIGHEST, preferred_element_type=F32
    )
    cum_row = lax.dot_general(
        log_decay, lower, (((1,), (1,)), ((), ())), precision=lax.Precision.HIGHEST, preferred_element_type=F32
    )
    row_ref[...] = cum_row
    col_ref[...] = cum_col
    end_ref[...] = jnp.exp(cum_row[:, rows - 1 : rows] - cum_row)
    hi, lo = split_hi_lo(jnp.exp(cum_col[rows - 1 : rows, :]))
    tail = jnp.concatenate([jnp.broadcast_to(hi, (8, LANES)), jnp.broadcast_to(lo, (8, LANES))], axis=0)
    copies[0].wait()
    copies[1].wait()
    for r in range(seqs):
        share = lax.rem(me + r, seqs)
        for j in range(per):
            h = share * per + j
            cols = pl.ds(pl.multiple_of(h * HEAD, HEAD), HEAD)
            keyed = (k_ref[:, cols].astype(F32).T * end_ref[pl.ds(h, 1), :]).astype(BF16)
            pieces[r][j * HEAD : (j + 1) * HEAD, :] = nn(keyed, v_ref[:, cols]).astype(BF16)
        pieces[r][per * HEAD : per * HEAD + PAD, :] = tail
    for copy in copies[3:]:
        copy.wait()


def pack_kernel(heads, router_ref, gain_ref, out_ref):
    experts = router_ref.shape[0]
    out_ref[0:experts, :] = router_ref[...]
    hi, lo = split_hi_lo(gain_ref[...])
    hi, lo = hi.astype(F32), lo.astype(F32)
    at = iota((PAD, HEAD), 0)
    for h in range(heads):
        both = jnp.where(at == 0, hi[h : h + 1, :], jnp.where(at == 1, lo[h : h + 1, :], 0.0))
        out_ref[experts : experts + PAD, h * HEAD : (h + 1) * HEAD] = both.astype(BF16)


def rows_kernel(
    heads, seqs, held, q_ref, k_ref, v_ref, res_ref, row_ref, col_ref, ids_ref, prio_ref, gate_ref, local_ref,
    grown_ref, place_ref, kept_ref, *pieces_and_sem,
):
    pieces, sem = pieces_and_sem[:-1], pieces_and_sem[-1]
    copy = pltpu.make_async_copy(gate_ref.at[:, pl.ds(0, kept_ref.shape[1]), :], kept_ref, sem)
    copy.start()
    place_kernel(held, ids_ref, prio_ref, place_ref)
    rows = q_ref.shape[0]
    causal = iota((rows, rows), 0) >= iota((rows, rows), 1)
    grow = jnp.exp(col_ref[...])
    for h in range(heads):
        cols = slice(h * HEAD, (h + 1) * HEAD)
        q = q_ref[:, cols]
        scores = nt(q, k_ref[:, cols])
        spread = col_ref[:, h : h + 1] - row_ref[h : h + 1, :]
        near = jnp.where(causal, scores * jnp.exp(jnp.where(causal, spread, 0.0)), 0.0).astype(BF16)
        local_ref[:, cols] = nn(near, v_ref[:, cols])
        grown_ref[:, cols] = (q.astype(F32) * grow[:, h : h + 1]).astype(BF16)
    place = place_ref[...]
    ids = ids_ref[...].astype(F32)
    lane = iota((held * CAP, LANES), 1)
    extra = jnp.zeros((held * CAP, LANES), F32)
    for i in range(ids.shape[0]):
        extra = jnp.where(lane == i, jnp.sum(place * ids[i : i + 1, :], axis=1, keepdims=True), extra)
    place = place.astype(BF16)
    me = lax.axis_index("seq")
    part = heads * HEAD // seqs
    for r in range(seqs):
        cols = pl.ds(pl.multiple_of(lax.rem(me + r, seqs) * part, part), part)
        pieces[r][:, 0:part] = nn(place, grown_ref[:, cols]).astype(BF16)
        pieces[r][:, part : 2 * part] = nn(place, local_ref[:, cols].astype(BF16)).astype(BF16)
        pieces[r][:, 2 * part : 3 * part] = nn(place, res_ref[:, cols]).astype(BF16)
        pieces[r][:, 3 * part : 3 * part + LANES] = extra.astype(BF16)
    copy.wait()


def keep_kernel(early, after_ref, gate_ref, up_ref, late_ref, kept_ref, sems):
    copies = (
        pltpu.make_async_copy(gate_ref.at[:, pl.ds(early, late_ref.shape[1]), :], late_ref, sems.at[0]),
        pltpu.make_async_copy(up_ref, kept_ref, sems.at[1]),
    )
    for copy in copies:
        copy.start()
    for copy in copies:
        copy.wait()


def owner_kernel(heads, seqs, held, again_ref, *refs):
    states, rows_in = refs[:seqs], refs[seqs : 2 * seqs]
    slots_ref, ids_ref, *rest = refs[2 * seqs :]
    prefixes, (state_ref, rows_ref, prefix_ref) = rest[:seqs], rest[seqs:]
    per = heads // seqs
    part = per * HEAD
    me = lax.axis_index("seq")
    expert = lax.axis_index("exp")
    for r in range(seqs):
        b = lax.rem(me + seqs - r, seqs)
        state_ref[b] = states[r][...]
        rows_ref[b] = rows_in[r][...]
        mine = rows_in[r][:, 3 * part : 3 * part + LANES].astype(F32)
        picked = jnp.zeros((CAP, LANES), F32)
        for e in range(held):
            picked = jnp.where(expert == e, mine[e * CAP : (e + 1) * CAP, :], picked)
        ids_ref[pl.ds(pl.multiple_of(b * CAP, CAP), CAP), :] = picked
    lane = iota((1, LANES), 1)
    for j in range(per):
        h = me * per + j
        again = again_ref[pl.ds(h, 1), :]
        cols = slice(j * HEAD, (j + 1) * HEAD)
        carry = jnp.zeros((HEAD, HEAD), F32)
        for b in range(seqs):
            prefix = carry.astype(BF16)
            prefix_ref[b, cols, :] = prefix
            attended = rows_ref[b, :, part + j * HEAD : part + (j + 1) * HEAD].astype(F32)
            if b > 0:
                attended = attended + nn(rows_ref[b, :, cols], prefix)
            power = jnp.mean(attended * attended, axis=1, keepdims=True)
            normed = attended * lax.rsqrt(power + EPS) * again
            residual = rows_ref[b, :, 2 * part + j * HEAD : 2 * part + (j + 1) * HEAD].astype(F32)
            mixed = (residual + normed).astype(BF16)
            for e in range(held):
                piece = mixed[e * CAP : (e + 1) * CAP, :]
                for s in range(seqs):
                    slots_ref[s, e, b * CAP : (b + 1) * CAP, cols] = piece
            if b + 1 < seqs:
                tail = state_ref[b, part : part + PAD, :].astype(F32)
                decay = jnp.where(lane == h, tail[0:1, :] + tail[8:9, :], 0.0)
                carry = jnp.sum(decay, axis=1, keepdims=True) * carry + state_ref[b, cols, :].astype(F32)
    for r in range(seqs):
        prefixes[r][...] = prefix_ref[lax.rem(me + r, seqs)]


def expert_in_kernel(seqs, held, width, in_ref, ids_ref, gate_early_ref, gate_late_ref, up_ref, *refs):
    tables, (down_ref, out_ref, share_ref, kept_ref, x_ref, sem) = refs[:held], refs[held:]
    copy = pltpu.make_async_copy(down_ref, kept_ref, sem)
    copy.start()
    part = in_ref.shape[2]
    slot_rows = in_ref.shape[1]
    experts = tables[0].shape[0] - PAD
    expert = lax.axis_index("exp")
    squares = jnp.zeros((slot_rows, 1), F32)
    for i in range(seqs * held):
        piece = in_ref[i].astype(F32)
        squares += jnp.sum(piece * piece, axis=1, keepdims=True)
    inverse = lax.rsqrt(squares / (held * width) + EPS)
    logits = jnp.zeros((slot_rows, experts), F32)
    for r in range(held):
        k = lax.rem(expert + held - r, held)
        for s in range(seqs):
            cols = slice(s * part, (s + 1) * part)
            gain = tables[r][experts : experts + PAD, cols].astype(F32)
            gain = gain[0:1, :] + gain[1:2, :]
            scaled = in_ref[s * held + k].astype(F32) * gain * inverse
            hi, lo = split_hi_lo(scaled)
            x_ref[:, pl.ds(pl.multiple_of(k * width + s * part, part), part)] = hi
            logits += nt(hi, tables[r][0:experts, cols]) + nt(lo, tables[r][0:experts, cols])
    probs = 1.0 / (1.0 + jnp.exp(-logits))
    lane = iota(probs.shape, 1)
    total = jnp.zeros((slot_rows, 1), F32)
    for i in range(2):
        number = ids_ref[:, i : i + 1].astype(jnp.int32)
        total += jnp.sum(jnp.where(lane == number, probs, 0.0), axis=1, keepdims=True)
    own = jnp.sum(jnp.where(lane == expert, probs, 0.0), axis=1, keepdims=True)
    share_ref[...] = jnp.broadcast_to(own / total, share_ref.shape)
    x = x_ref[...]
    early = gate_early_ref.shape[1]
    gate = nn(x[:, 0:early], gate_early_ref[0]) + nn(x[:, early:], gate_late_ref[0])
    up = nn(x, up_ref[0])
    out_ref[...] = (gate * (1.0 / (1.0 + jnp.exp(-gate))) * up).astype(BF16)
    copy.wait()


def expert_out_kernel(seqs, held, w_ref, share_ref, *refs):
    h_refs, out_refs, acc_ref = refs[:seqs], refs[seqs : seqs + held], refs[seqs + held]
    part = h_refs[0].shape[-1]
    me, expert = lax.axis_index("seq"), lax.axis_index("exp")
    total = None
    for r in range(seqs):
        at = pl.multiple_of(lax.rem(me + seqs - r, seqs) * part, part)
        term = nn(h_refs[r][...], w_ref[0, pl.ds(at, part), :])
        total = term if total is None else total + term
    acc_ref[...] = total * share_ref[:, 0:1]
    for r in range(held):
        at = pl.multiple_of(lax.rem(expert + r, seqs) * CAP, CAP)
        out_refs[r][...] = acc_ref[pl.ds(at, CAP), :].astype(BF16)


def mixed_kernel(heads, seqs, grown_ref, local_ref, res_ref, again_ref, *refs):
    prefixes, mixed_ref = refs[:seqs], refs[seqs]
    me = lax.axis_index("seq")
    per = heads // seqs
    for r in range(seqs):
        share = lax.rem(me + seqs - r, seqs)
        for j in range(per):
            h = share * per + j
            cols = pl.ds(pl.multiple_of(h * HEAD, HEAD), HEAD)
            inter = nn(grown_ref[:, cols], prefixes[r][j * HEAD : (j + 1) * HEAD, :])
            attended = local_ref[:, cols] + inter
            power = jnp.mean(attended * attended, axis=1, keepdims=True)
            normed = attended * lax.rsqrt(power + EPS) * again_ref[pl.ds(h, 1), :]
            mixed_ref[:, cols] = (res_ref[:, cols].astype(F32) + normed).astype(BF16)


def add_kernel(held, mixed_ref, place_ref, *refs):
    y_refs, out_ref, y_ref = refs[:held], refs[held], refs[held + 1]
    me = lax.axis_index("seq")
    for r, ref in enumerate(y_refs):
        at = pl.multiple_of(lax.rem(me + held - r, held) * CAP, CAP)
        y_ref[pl.ds(at, CAP), :] = ref[...].astype(F32)
    extra = tn(place_ref[...].astype(BF16), y_ref[...].astype(BF16))
    out_ref[...] = (mixed_ref[...].astype(F32) + extra).astype(BF16)


def run(body, out_shape, args, scratch=(), flops=1000, nbytes=1000, vmem=SMALL, anywhere=0):
    outs = out_shape if isinstance(out_shape, tuple) else (out_shape,)
    specs = tuple(VMEM for _ in outs)
    kernel = pl.pallas_call(
        body,
        out_shape=out_shape,
        in_specs=[VMEM] * (len(args) - anywhere) + [pl.BlockSpec(memory_space=pltpu.HBM)] * anywhere,
        out_specs=specs if isinstance(out_shape, tuple) else specs[0],
        scratch_shapes=list(scratch),
        compiler_params=pltpu.CompilerParams(vmem_limit_bytes=vmem),
        cost_estimate=pl.CostEstimate(flops=flops, bytes_accessed=nbytes, transcendentals=0),
    )
    near = len(args) - anywhere
    return kernel(*args[:near], *(pltpu.with_memory_space_constraint(x, pltpu.HBM) for x in args[near:]))


def rotate(x, axis, count, step):
    return lax.ppermute(x, axis, [(i, (i + step) % count) for i in range(count)])


def spread(pieces, axis, count):
    return [pieces[0]] + [rotate(pieces[r], axis, count, r) for r in range(1, count)]


def ring_body(
    residual, query_rows, key_rows, value_rows, log_decay, attn_gain, norm_gain, router, expert_ids, priority,
    gate_weight, up_weight, down_weight,
):
    rows, width = residual.shape
    heads = width // HEAD
    held = lax.axis_size("exp")
    seqs = lax.axis_size("seq")
    experts = router.shape[1]
    part = width // seqs
    slot_rows = seqs * CAP
    hidden_part = gate_weight.shape[2]
    out_part = down_weight.shape[2]
    small = (
        key_rows, value_rows, log_decay.T, query_rows, residual, expert_ids.T, priority, router.T,
        norm_gain.reshape(heads, HEAD), attn_gain.reshape(heads, HEAD),
    )
    *outs, cum_row, cum_col = run(
        functools.partial(state_pieces_kernel, heads, seqs, len(small)),
        (
            *(pltpu.VMEM(x.shape, x.dtype) for x in small),
            *(shaped((part + PAD, LANES), BF16) for _ in range(seqs)),
            shaped((LANES, rows), F32),
            shaped((rows, LANES), F32),
        ),
        small,
        scratch=[
            pltpu.VMEM((LANES, rows), F32),
            pltpu.VMEM((LANES, rows), F32),
            pltpu.SemaphoreType.DMA((len(small),)),
        ],
        anywhere=len(small),
    )
    keys, values, _, queries, stream, ids, order, router_rows, gain, again = outs[: len(small)]
    pieces = outs[len(small) :]
    states = spread(pieces, "seq", seqs)
    table = run(functools.partial(pack_kernel, heads), shaped((experts + PAD, width), BF16), (router_rows, gain))
    tables = spread([table] * held, "exp", held)
    early = held * width // 2
    local, grown, place, gate_early, *row_pieces = run(
        functools.partial(rows_kernel, heads, seqs, held),
        (
            shaped((rows, width), F32),
            shaped((rows, width), BF16),
            shaped((held * CAP, rows), F32),
            pltpu.VMEM((1, early, hidden_part), BF16),
            *(shaped((held * CAP, 3 * part + LANES), BF16) for _ in range(seqs)),
        ),
        (queries, keys, values, stream, cum_row, cum_col, ids, order, gate_weight),
        scratch=[pltpu.SemaphoreType.DMA],
        flops=200_000_000,
        nbytes=9_000_000,
        anywhere=1,
    )
    row_parts = spread(row_pieces, "seq", seqs)
    gate_late, up_kept = run(
        functools.partial(keep_kernel, early),
        (
            pltpu.VMEM((1, held * width - early, hidden_part), BF16),
            pltpu.VMEM(up_weight.shape, BF16),
        ),
        (row_pieces[0], gate_weight, up_weight),
        scratch=[pltpu.SemaphoreType.DMA((2,))],
        nbytes=21_000_000,
        anywhere=2,
    )
    slots, slot_ids, *prefixes = run(
        functools.partial(owner_kernel, heads, seqs, held),
        (
            pltpu.VMEM((seqs, held, slot_rows, part), BF16),
            shaped((slot_rows, LANES), F32),
            *(shaped((part, LANES), BF16) for _ in range(seqs)),
        ),
        (again, *states, *row_parts),
        scratch=[
            pltpu.VMEM((seqs, part + PAD, LANES), BF16),
            pltpu.VMEM((seqs, held * CAP, 3 * part + LANES), BF16),
            pltpu.VMEM((seqs, part, LANES), BF16),
        ],
    )
    slots = slots.reshape(seqs * held, slot_rows, part)
    gathered = lax.all_to_all(slots, ("seq", "exp"), split_axis=0, concat_axis=0, tiled=True)
    hidden, shares, down_kept = run(
        functools.partial(expert_in_kernel, seqs, held, width),
        (
            shaped((slot_rows, hidden_part), BF16),
            shaped((slot_rows, LANES), F32),
            pltpu.VMEM(down_weight.shape, BF16),
        ),
        (gathered, slot_ids, gate_early, gate_late, up_kept, *tables, down_weight),
        scratch=[pltpu.VMEM((slot_rows, held * width), BF16), pltpu.SemaphoreType.DMA],
        flops=900_000_000,
        nbytes=28_000_000,
        anywhere=1,
    )
    hiddens = spread([hidden] * seqs, "seq", seqs)
    prefixes, hidden = lax.optimization_barrier((prefixes, hidden))
    returned = spread(prefixes, "seq", seqs)
    outs = run(
        functools.partial(expert_out_kernel, seqs, held),
        (shaped((CAP, out_part), BF16),) * held,
        (down_kept, shares, *hiddens),
        scratch=[pltpu.VMEM((slot_rows, out_part), F32)],
        flops=450_000_000,
        nbytes=14_000_000,
    )
    y = [
        lax.ppermute(
            piece,
            ("seq", "exp"),
            [(s * held + e, ((e + r) % seqs) * held + s) for s in range(seqs) for e in range(held)],
        )
        for r, piece in enumerate(outs)
    ]
    mixed = run(
        functools.partial(mixed_kernel, heads, seqs),
        shaped((rows, width), BF16),
        (grown, local, stream, again, *returned),
        flops=100_000_000,
        nbytes=2_000_000,
    )
    return run(
        functools.partial(add_kernel, held),
        shaped((rows, width), BF16),
        (mixed, place, *y),
        scratch=[pltpu.VMEM((held * CAP, width), F32)],
    )


def body(residual, *args):
    seqs, held = lax.axis_size("seq"), lax.axis_size("exp")
    if seqs == held and (residual.shape[1] // HEAD) % seqs == 0:
        return ring_body(residual, *args)
    return general_body(residual, *args)


def solution(mesh):
    token = P(("groups", "seq"), "exp")
    return jax.shard_map(
        body,
        mesh=mesh,
        in_specs=(
            token, token, token, token, token, P("exp"), P("exp"), P("exp", None),
            P(("groups", "seq"), None), P(("groups", "seq"), None),
            P("exp", None, "seq"), P("exp", None, "seq"), P("exp", None, "seq"),
        ),
        out_specs=token,
        check_vma=False,
    )
```

```python
import functools

import jax
import jax.numpy as jnp
from jax import lax
from jax.experimental import pallas as pl
from jax.experimental.pallas import tpu as pltpu
from jax.sharding import PartitionSpec as P


HEAD = 128
LANES = 128
CAP = 8
PAD = 16
EPS = 1e-06
SMALL = 8 << 20
F32 = jnp.float32
BF16 = jnp.bfloat16


VMEM = pl.BlockSpec(memory_space=pltpu.VMEM)


def nt(a, b):
    return lax.dot_general(a, b, (((1,), (1,)), ((), ())), preferred_element_type=F32)


def tn(a, b):
    return lax.dot_general(a, b, (((0,), (0,)), ((), ())), preferred_element_type=F32)


def nn(a, b):
    return lax.dot_general(a, b, (((1,), (0,)), ((), ())), preferred_element_type=F32)


def iota(shape, dim):
    return lax.broadcasted_iota(jnp.int32, shape, dim)


def split_hi_lo(x):
    hi = x.astype(BF16)
    return hi, (x - hi.astype(F32)).astype(BF16)


def state_kernel(heads, shares, share_rows, k_ref, v_ref, decay_ref, pay_ref, row_ref, col_ref, pad_ref):
    rows = k_ref.shape[0]
    pad_ref[...] = jnp.zeros_like(pad_ref)
    pad_ref[0:heads, :] = decay_ref[...]
    log_decay = pad_ref[...]
    lower = jnp.where(iota((rows, rows), 0) >= iota((rows, rows), 1), 1.0, 0.0).astype(F32)
    cum_col = lax.dot_general(
        lower, log_decay, (((1,), (1,)), ((), ())), precision=lax.Precision.HIGHEST, preferred_element_type=F32
    )
    cum_row = lax.dot_general(
        log_decay, lower, (((1,), (1,)), ((), ())), precision=lax.Precision.HIGHEST, preferred_element_type=F32
    )
    row_ref[...] = cum_row
    col_ref[...] = cum_col
    to_end = jnp.exp(cum_col[rows - 1 : rows, :] - cum_col)
    hi, lo = split_hi_lo(jnp.exp(cum_col[rows - 1 : rows, :]))
    for s in range(shares):
        pay_ref[s, share_rows : share_rows + PAD, :] = jnp.concatenate(
            [jnp.broadcast_to(hi, (8, LANES)), jnp.broadcast_to(lo, (8, LANES))], axis=0
        )
    for h in range(heads):
        cols = slice(h * HEAD, (h + 1) * HEAD)
        keyed = (k_ref[:, cols].astype(F32) * to_end[:, h : h + 1]).astype(BF16)
        state = tn(keyed, v_ref[:, cols]).astype(BF16)
        at = h * HEAD
        while at < (h + 1) * HEAD:
            share, inner = divmod(at, share_rows)
            take = min(share_rows - inner, (h + 1) * HEAD - at)
            pay_ref[share, inner : inner + take, :] = state[at - h * HEAD : at - h * HEAD + take, :]
            at += take


def local_kernel(heads, q_ref, k_ref, v_ref, row_ref, col_ref, out_ref):
    rows = q_ref.shape[0]
    causal = iota((rows, rows), 0) >= iota((rows, rows), 1)
    for h in range(heads):
        cols = slice(h * HEAD, (h + 1) * HEAD)
        scores = nt(q_ref[:, cols], k_ref[:, cols])
        spread = col_ref[:, h : h + 1] - row_ref[h : h + 1, :]
        weights = jnp.where(causal, scores * jnp.exp(jnp.where(causal, spread, 0.0)), 0.0).astype(BF16)
        out_ref[:, cols] = nn(weights, v_ref[:, cols])


def place_kernel(held, ids_ref, prio_ref, place_ref):
    rows = ids_ref.shape[1]
    order = prio_ref[...].astype(F32)
    across = jnp.broadcast_to(order, (rows, rows))
    earlier = jnp.where(across.T < across, 1.0, 0.0).astype(BF16)
    ids = ids_ref[...]
    expert = iota((8 * pl.cdiv(held, 8), rows), 0)
    hit = expert == ids[0:1, :]
    for i in range(1, ids.shape[0]):
        hit = hit | (expert == ids[i : i + 1, :])
    member = jnp.where(hit, 1.0, 0.0)
    rank = nn(member.astype(BF16), earlier)
    slot = iota((CAP, rows), 0).astype(F32)
    for e in range(held):
        chosen = (member[e : e + 1, :] > 0.5) & (rank[e : e + 1, :] == slot)
        place_ref[e * CAP : (e + 1) * CAP, :] = jnp.where(chosen, 1.0, 0.0)


def scan_kernel(shares, share_rows, in_ref, out_ref):
    me = lax.axis_index("seq")
    row = me * share_rows + iota((share_rows, LANES), 0)
    onehot = jnp.where(row // HEAD == iota((share_rows, LANES), 1), 1.0, 0.0)
    carry = jnp.zeros((share_rows, LANES), F32)
    for b in range(shares):
        out_ref[b, :, :] = carry.astype(BF16)
        if b + 1 < shares:
            tail = in_ref[b, share_rows : share_rows + PAD, :].astype(F32)
            decay = tail[0:1, :] + tail[8:9, :]
            each = jnp.sum(onehot * decay, axis=1, keepdims=True)
            carry = each * carry + in_ref[b, 0:share_rows, :].astype(F32)


def mix_kernel(
    heads, held, copies, q_ref, local_ref, carried_ref, col_ref, res_ref, again_ref, ngain_ref, router_ref, place_ref,
    mixed_ref, slots_ref, stats_ref,
):
    rows = q_ref.shape[0]
    width = heads * HEAD
    experts = router_ref.shape[0]
    place = place_ref[...].astype(BF16)
    grow = jnp.exp(col_ref[...])
    squares = jnp.zeros((rows, 1), F32)
    picked_squares = jnp.zeros((held * CAP, 1), F32)
    logits = jnp.zeros((experts, rows), F32)
    for h in range(heads):
        cols = slice(h * HEAD, (h + 1) * HEAD)
        inter = nn(q_ref[:, cols], carried_ref[h * HEAD : (h + 1) * HEAD, :])
        attended = local_ref[:, cols] + grow[:, h : h + 1] * inter
        power = jnp.mean(attended * attended, axis=1, keepdims=True)
        normed = attended * lax.rsqrt(power + EPS) * again_ref[:, cols]
        mixed = (res_ref[:, cols].astype(F32) + normed).astype(BF16)
        mixed_ref[:, cols] = mixed
        mixed_f = mixed.astype(F32)
        squares += jnp.sum(mixed_f * mixed_f, axis=1, keepdims=True)
        hi, lo = split_hi_lo(mixed_f * ngain_ref[:, cols])
        logits += nt(router_ref[:, cols], hi) + nt(router_ref[:, cols], lo)
        picked = nn(place, mixed)
        picked_squares += jnp.sum(picked * picked, axis=1, keepdims=True)
        sent = (picked * ngain_ref[:, cols]).astype(BF16)
        for s in range(copies):
            for e in range(held):
                slots_ref[s, e, :, cols] = sent[e * CAP : (e + 1) * CAP, :]
    lane = iota((held * CAP, LANES), 1)
    hi, lo = split_hi_lo(picked_squares)
    extra = jnp.where(lane == 0, hi.astype(F32), jnp.where(lane == 1, lo.astype(F32), 0.0)).astype(BF16)
    for s in range(copies):
        for e in range(held):
            slots_ref[s, e, :, width : width + LANES] = extra[e * CAP : (e + 1) * CAP, :]
    stats_ref[0:experts, :] = logits
    stats_ref[experts : experts + 8, :] = jnp.broadcast_to(squares, (rows, rows)).T[0:8, :]


def gate_up_kernel(seqs, held, width, chunk, in_ref, gate_ref, up_ref, out_ref, x_ref, acc_g, acc_u):
    step = pl.program_id(0)
    per = width // chunk

    @pl.when(step == 0)
    def _():
        for s in range(seqs):
            for k in range(held):
                for p in range(per):
                    x_ref[k * per + p, s * CAP : (s + 1) * CAP, :] = in_ref[s * held + k, :, p * chunk : (p + 1) * chunk]
        acc_g[...] = jnp.zeros_like(acc_g)
        acc_u[...] = jnp.zeros_like(acc_u)

    x = x_ref[step]
    acc_g[...] += nn(x, gate_ref[0])
    acc_u[...] += nn(x, up_ref[0])

    @pl.when(step == pl.num_programs(0) - 1)
    def _():
        parts = []
        for s in range(seqs):
            total = jnp.zeros((CAP, 1), F32)
            for k in range(held):
                tail = in_ref[s * held + k, :, width : width + LANES].astype(F32)
                total += tail[:, 0:1] + tail[:, 1:2]
            parts.append(total)
        squares = jnp.concatenate(parts, axis=0)
        inverse = lax.rsqrt(squares / (held * width) + EPS)
        gate = acc_g[...] * inverse
        up = acc_u[...] * inverse
        out_ref[...] = (gate * (1.0 / (1.0 + jnp.exp(-gate))) * up).astype(BF16)


def down_kernel(seqs, order_ref, h_ref, w_ref, out_ref, acc):
    step = pl.program_id(0)

    @pl.when(step == 0)
    def _():
        acc[...] = jnp.zeros_like(acc)

    acc[...] += nn(h_ref[0], w_ref[0])

    @pl.when(step == pl.num_programs(0) - 1)
    def _():
        for s in range(seqs):
            out_ref[s, :, :] = acc[s * CAP : (s + 1) * CAP, :].astype(BF16)


def gates_kernel(held, total_width, parts, *refs):
    stats_refs, (ids_ref, place_ref, hi_ref, lo_ref) = refs[:parts], refs[parts:]
    total = stats_refs[0][...]
    for ref in stats_refs[1:]:
        total = total + ref[...]
    experts = total.shape[0] - 8
    inverse = lax.rsqrt(total[experts : experts + 1, :] / total_width + EPS)
    logits = total[0:experts, :] * inverse
    probs = 1.0 / (1.0 + jnp.exp(-logits))
    expert = iota(probs.shape, 0)
    ids = ids_ref[...]
    chosen = [
        jnp.sum(jnp.where(expert == ids[i : i + 1, :], probs, 0.0), axis=0, keepdims=True) for i in range(ids.shape[0])
    ]
    norm = chosen[0]
    for c in chosen[1:]:
        norm = norm + c
    for e in range(held):
        gate = jnp.zeros_like(norm)
        for i, c in enumerate(chosen):
            gate += jnp.where(ids[i : i + 1, :] == e, c / norm, 0.0)
        hi, lo = split_hi_lo(place_ref[e * CAP : (e + 1) * CAP, :] * gate)
        hi_ref[e * CAP : (e + 1) * CAP, :] = hi.astype(F32)
        lo_ref[e * CAP : (e + 1) * CAP, :] = lo.astype(F32)


def combine_kernel(held, mixed_ref, hi_ref, lo_ref, *refs):
    y_refs, out_ref = refs[:-1], refs[-1]
    if len(y_refs) > 1:
        y = jnp.concatenate([r[...].astype(F32) for r in y_refs], axis=0).astype(BF16)
    else:
        y = jnp.concatenate([y_refs[0][e].astype(F32) for e in range(held)], axis=0).astype(BF16)
    extra = tn(hi_ref[...].astype(BF16), y) + tn(lo_ref[...].astype(BF16), y)
    out_ref[...] = (mixed_ref[...].astype(F32) + extra).astype(BF16)


def call(body, out_shape, args, scratch=(), flops=0, nbytes=0):
    return pl.pallas_call(
        body,
        out_shape=out_shape,
        in_specs=[VMEM] * len(args),
        out_specs=jax.tree.map(lambda _: VMEM, out_shape),
        scratch_shapes=list(scratch),
        cost_estimate=pl.CostEstimate(flops=flops or 1000, bytes_accessed=nbytes or 1000, transcendentals=0),
    )(*args)


def shaped(shape, dtype):
    return jax.ShapeDtypeStruct(shape, dtype)


def general_body(
    residual, query_rows, key_rows, value_rows, log_decay, attn_gain, norm_gain, router, expert_ids, priority,
    gate_weight, up_weight, down_weight,
):
    rows, width = residual.shape
    heads = width // HEAD
    held = lax.axis_size("exp")
    seqs = lax.axis_size("seq")
    experts = router.shape[1]
    share_rows = width // seqs
    hidden_part = gate_weight.shape[2]
    out_part = down_weight.shape[2]
    ids = expert_ids.T
    payload, cum_row, cum_col = call(
        functools.partial(state_kernel, heads, seqs, share_rows),
        (
            shaped((seqs, share_rows + PAD, LANES), BF16),
            shaped((LANES, rows), F32),
            shaped((rows, LANES), F32),
        ),
        (key_rows, value_rows, log_decay.T),
        scratch=[pltpu.VMEM((LANES, rows), F32)],
        flops=60_000_000,
        nbytes=1_200_000,
    )
    arrived = lax.all_to_all(payload, "seq", split_axis=0, concat_axis=0, tiled=True)
    local = call(
        functools.partial(local_kernel, heads),
        shaped((rows, width), F32),
        (query_rows, key_rows, value_rows, cum_row, cum_col),
        flops=200_000_000,
        nbytes=2_000_000,
    )
    place = call(functools.partial(place_kernel, held), shaped((held * CAP, rows), F32), (ids, priority))
    prefix = call(functools.partial(scan_kernel, seqs, share_rows), shaped((seqs, share_rows, LANES), BF16), (arrived,))
    carried = lax.all_to_all(prefix, "seq", split_axis=0, concat_axis=0, tiled=True).reshape(width, LANES)
    mixed, slots, stats = call(
        functools.partial(mix_kernel, heads, held, seqs),
        (
            shaped((rows, width), BF16),
            shaped((seqs, held, CAP, width + LANES), BF16),
            shaped((experts + 8, rows), F32),
        ),
        (
            query_rows, local, carried, cum_col, residual, attn_gain[None], norm_gain[None], router.T, place,
        ),
        flops=200_000_000,
        nbytes=3_000_000,
    )
    slots = slots.reshape(seqs * held, CAP, width + LANES)
    gathered = lax.all_to_all(slots, ("seq", "exp"), split_axis=0, concat_axis=0, tiled=True)
    stat_parts = [stats]
    for r in range(1, held):
        stat_parts.append(lax.ppermute(stats, "exp", [(i, (i + r) % held) for i in range(held)]))
    slot_rows = seqs * CAP
    chunk = width // 2
    hidden = pl.pallas_call(
        functools.partial(gate_up_kernel, seqs, held, width, chunk),
        out_shape=shaped((slot_rows, hidden_part), BF16),
        grid=(held * width // chunk,),
        in_specs=[
            VMEM,
            pl.BlockSpec((1, chunk, hidden_part), lambda i: (0, i, 0)),
            pl.BlockSpec((1, chunk, hidden_part), lambda i: (0, i, 0)),
        ],
        out_specs=pl.BlockSpec((slot_rows, hidden_part), lambda i: (0, 0)),
        scratch_shapes=[
            pltpu.VMEM((held * width // chunk, slot_rows, chunk), BF16),
            pltpu.VMEM((slot_rows, hidden_part), F32),
            pltpu.VMEM((slot_rows, hidden_part), F32),
        ],
        name="gate_up",
        cost_estimate=pl.CostEstimate(flops=900_000_000, bytes_accessed=28_000_000, transcendentals=0),
    )(gathered, gate_weight, up_weight)
    me = lax.axis_index("seq")
    if seqs <= 8:
        parts = [hidden]
        for r in range(1, seqs):
            parts.append(lax.ppermute(hidden, "seq", [(i, (i + r) % seqs) for i in range(seqs)]))
        whole = jnp.stack(parts)
        order = jnp.mod(me - jnp.arange(seqs, dtype=jnp.int32), seqs)
    else:
        whole = lax.all_gather(hidden, "seq", axis=0)
        order = jnp.arange(seqs, dtype=jnp.int32)
    expert_out = pl.pallas_call(
        functools.partial(down_kernel, seqs),
        out_shape=shaped((seqs, CAP, out_part), BF16),
        grid_spec=pltpu.PrefetchScalarGridSpec(
            num_scalar_prefetch=1,
            grid=(seqs,),
            in_specs=[
                pl.BlockSpec((1, slot_rows, hidden_part), lambda i, o: (i, 0, 0)),
                pl.BlockSpec((1, hidden_part, out_part), lambda i, o: (0, o[i], 0)),
            ],
            out_specs=pl.BlockSpec((seqs, CAP, out_part), lambda i, o: (0, 0, 0)),
            scratch_shapes=[pltpu.VMEM((slot_rows, out_part), F32)],
        ),
        name="down",
        cost_estimate=pl.CostEstimate(flops=450_000_000, bytes_accessed=14_000_000, transcendentals=0),
    )(order, whole, down_weight)
    if seqs == held:
        pieces = []
        for r in range(seqs):
            target = [
                (s * held + e, ((e + r) % seqs) * held + s) for s in range(seqs) for e in range(held)
            ]
            mine = lax.dynamic_index_in_dim(
                expert_out, jnp.mod(lax.axis_index("exp") + r, seqs), axis=0, keepdims=False
            )
            pieces.append(lax.ppermute(mine, ("seq", "exp"), target))
        stacked = jnp.stack(pieces)
        source = jnp.mod(me - jnp.arange(held, dtype=jnp.int32), held)
        y = (jnp.take(stacked, source, axis=0),)
    else:
        returned = lax.all_to_all(expert_out, "seq", split_axis=0, concat_axis=1, tiled=True)
        returned = returned.reshape(CAP, seqs * out_part)
        y = (lax.all_to_all(returned[None], "exp", split_axis=2, concat_axis=0, tiled=True),)
    hi, lo = call(
        functools.partial(gates_kernel, held, held * width, len(stat_parts)),
        (shaped((held * CAP, rows), F32),) * 2,
        (*stat_parts, ids, place),
    )
    return call(functools.partial(combine_kernel, held), shaped((rows, width), BF16), (mixed, hi, lo, *y))


def state_pieces_kernel(heads, seqs, count, *refs):
    sources, kept, refs = refs[:count], refs[count : 2 * count], refs[2 * count :]
    pieces, row_ref, col_ref, pad_ref, end_ref, sems = refs[:seqs], *refs[seqs:]
    copies = [pltpu.make_async_copy(a, b, sems.at[i]) for i, (a, b) in enumerate(zip(sources, kept))]
    for copy in copies:
        copy.start()
    k_ref, v_ref, decay_ref = kept[:3]
    copies[2].wait()
    rows = k_ref.shape[0]
    per = heads // seqs
    me = lax.axis_index("seq")
    pad_ref[...] = jnp.zeros_like(pad_ref)
    pad_ref[0:heads, :] = decay_ref[...]
    log_decay = pad_ref[...]
    lower = jnp.where(iota((rows, rows), 0) >= iota((rows, rows), 1), 1.0, 0.0).astype(F32)
    cum_col = lax.dot_general(
        lower, log_decay, (((1,), (1,)), ((), ())), precision=lax.Precision.HIGHEST, preferred_element_type=F32
    )
    cum_row = lax.dot_general(
        log_decay, lower, (((1,), (1,)), ((), ())), precision=lax.Precision.HIGHEST, preferred_element_type=F32
    )
    row_ref[...] = cum_row
    col_ref[...] = cum_col
    end_ref[...] = jnp.exp(cum_row[:, rows - 1 : rows] - cum_row)
    hi, lo = split_hi_lo(jnp.exp(cum_col[rows - 1 : rows, :]))
    tail = jnp.concatenate([jnp.broadcast_to(hi, (8, LANES)), jnp.broadcast_to(lo, (8, LANES))], axis=0)
    copies[0].wait()
    copies[1].wait()
    for r in range(seqs):
        share = lax.rem(me + r, seqs)
        for j in range(per):
            h = share * per + j
            cols = pl.ds(pl.multiple_of(h * HEAD, HEAD), HEAD)
            keyed = (k_ref[:, cols].astype(F32).T * end_ref[pl.ds(h, 1), :]).astype(BF16)
            pieces[r][j * HEAD : (j + 1) * HEAD, :] = nn(keyed, v_ref[:, cols]).astype(BF16)
        pieces[r][per * HEAD : per * HEAD + PAD, :] = tail
    for copy in copies[3:]:
        copy.wait()


def pack_kernel(heads, router_ref, gain_ref, out_ref):
    experts = router_ref.shape[0]
    out_ref[0:experts, :] = router_ref[...]
    hi, lo = split_hi_lo(gain_ref[...])
    hi, lo = hi.astype(F32), lo.astype(F32)
    at = iota((PAD, HEAD), 0)
    for h in range(heads):
        both = jnp.where(at == 0, hi[h : h + 1, :], jnp.where(at == 1, lo[h : h + 1, :], 0.0))
        out_ref[experts : experts + PAD, h * HEAD : (h + 1) * HEAD] = both.astype(BF16)


def rows_kernel(
    heads, seqs, held, q_ref, k_ref, v_ref, res_ref, row_ref, col_ref, ids_ref, prio_ref, local_ref,
    grown_ref, place_ref, *pieces,
):
    place_kernel(held, ids_ref, prio_ref, place_ref)
    rows = q_ref.shape[0]
    causal = iota((rows, rows), 0) >= iota((rows, rows), 1)
    grow = jnp.exp(col_ref[...])
    for h in range(heads):
        cols = slice(h * HEAD, (h + 1) * HEAD)
        q = q_ref[:, cols]
        scores = nt(q, k_ref[:, cols])
        spread = col_ref[:, h : h + 1] - row_ref[h : h + 1, :]
        near = jnp.where(causal, scores * jnp.exp(jnp.where(causal, spread, 0.0)), 0.0).astype(BF16)
        local_ref[:, cols] = nn(near, v_ref[:, cols])
        grown_ref[:, cols] = (q.astype(F32) * grow[:, h : h + 1]).astype(BF16)
    place = place_ref[...]
    ids = ids_ref[...].astype(F32)
    lane = iota((held * CAP, LANES), 1)
    extra = jnp.zeros((held * CAP, LANES), F32)
    for i in range(ids.shape[0]):
        extra = jnp.where(lane == i, jnp.sum(place * ids[i : i + 1, :], axis=1, keepdims=True), extra)
    place = place.astype(BF16)
    me = lax.axis_index("seq")
    part = heads * HEAD // seqs
    for r in range(seqs):
        cols = pl.ds(pl.multiple_of(lax.rem(me + r, seqs) * part, part), part)
        pieces[r][:, 0:part] = nn(place, grown_ref[:, cols]).astype(BF16)
        pieces[r][:, part : 2 * part] = nn(place, local_ref[:, cols].astype(BF16)).astype(BF16)
        pieces[r][:, 2 * part : 3 * part] = nn(place, res_ref[:, cols]).astype(BF16)
        pieces[r][:, 3 * part : 3 * part + LANES] = extra.astype(BF16)


def copy_rows(source, start, target, sem):
    return pltpu.make_async_copy(source.at[:, pl.ds(start, target.shape[1]), :], target, sem)


def keep_kernel(starts, after_ref, *refs):
    count = len(starts)
    copies = [
        copy_rows(refs[i], starts[i], refs[count + i], refs[2 * count].at[i]) for i in range(count)
    ]
    for copy in copies:
        copy.start()
    for copy in copies:
        copy.wait()


def owner_kernel(heads, seqs, held, again_ref, *refs):
    states, rows_in = refs[:seqs], refs[seqs : 2 * seqs]
    slots_refs, ids_ref, *rest = refs[2 * seqs : 2 * seqs + held], *refs[2 * seqs + held :]
    prefixes, (state_ref, rows_ref, prefix_ref, mixed_ref) = rest[:seqs], rest[seqs:]
    per = heads // seqs
    part = per * HEAD
    me = lax.axis_index("seq")
    expert = lax.axis_index("exp")
    for r in range(seqs):
        b = lax.rem(me + seqs - r, seqs)
        state_ref[b] = states[r][...]
        rows_ref[b] = rows_in[r][...]
        mine = rows_in[r][:, 3 * part : 3 * part + LANES].astype(F32)
        picked = jnp.zeros((CAP, LANES), F32)
        for e in range(held):
            picked = jnp.where(expert == e, mine[e * CAP : (e + 1) * CAP, :], picked)
        ids_ref[pl.ds(pl.multiple_of(b * CAP, CAP), CAP), :] = picked
    lane = iota((1, LANES), 1)
    for j in range(per):
        h = me * per + j
        again = again_ref[pl.ds(h, 1), :]
        cols = slice(j * HEAD, (j + 1) * HEAD)
        carry = jnp.zeros((HEAD, HEAD), F32)
        for b in range(seqs):
            prefix = carry.astype(BF16)
            prefix_ref[b, cols, :] = prefix
            attended = rows_ref[b, :, part + j * HEAD : part + (j + 1) * HEAD].astype(F32)
            if b > 0:
                attended = attended + nn(rows_ref[b, :, cols], prefix)
            power = jnp.mean(attended * attended, axis=1, keepdims=True)
            normed = attended * lax.rsqrt(power + EPS) * again
            residual = rows_ref[b, :, 2 * part + j * HEAD : 2 * part + (j + 1) * HEAD].astype(F32)
            mixed_ref[b, :, cols] = residual + normed
            if b + 1 < seqs:
                tail = state_ref[b, part : part + PAD, :].astype(F32)
                decay = jnp.where(lane == h, tail[0:1, :] + tail[8:9, :], 0.0)
                carry = jnp.sum(decay, axis=1, keepdims=True) * carry + state_ref[b, cols, :].astype(F32)
    for r in range(held):
        at = pl.ds(pl.multiple_of(lax.rem(expert + r, held) * CAP, CAP), CAP)
        slots_refs[r][...] = jnp.concatenate([mixed_ref[b, at, :] for b in range(seqs)], axis=0).astype(BF16)
    for r in range(seqs):
        prefixes[r][...] = prefix_ref[lax.rem(me + r, seqs)]


def join_kernel(*refs):
    for r, ref in enumerate(refs[:-1]):
        refs[-1][r] = ref[...]


def expert_in_kernel(seqs, held, width, ids_ref, gate_ref, up_ref, *refs):
    gathered, tables, refs = refs[:seqs], refs[seqs : seqs + held], refs[seqs + held :]
    down_ref, out_ref, share_ref, kept_ref, x_ref, sem = refs
    copy = pltpu.make_async_copy(down_ref, kept_ref, sem)
    copy.start()
    slot_rows, part = gathered[0].shape[1:]
    experts = tables[0].shape[0] - PAD
    me, expert = lax.axis_index("seq"), lax.axis_index("exp")
    squares = jnp.zeros((slot_rows, 1), F32)
    for source in gathered:
        for r in range(held):
            piece = source[r].astype(F32)
            squares += jnp.sum(piece * piece, axis=1, keepdims=True)
    inverse = lax.rsqrt(squares / (held * width) + EPS)
    logits = jnp.zeros((slot_rows, experts), F32)
    for r in range(held):
        k = lax.rem(expert + held - r, held)
        for i in range(seqs):
            start = pl.multiple_of(lax.rem(me + seqs - i, seqs) * part, part)
            cols = pl.ds(start, part)
            gain = tables[r][experts : experts + PAD, cols].astype(F32)
            gain = gain[0:1, :] + gain[1:2, :]
            hi, lo = split_hi_lo(gathered[i][r].astype(F32) * gain * inverse)
            x_ref[:, pl.ds(pl.multiple_of(k * width + start, part), part)] = hi
            logits += nt(hi, tables[r][0:experts, cols]) + nt(lo, tables[r][0:experts, cols])
    probs = 1.0 / (1.0 + jnp.exp(-logits))
    lane = iota(probs.shape, 1)
    total = jnp.zeros((slot_rows, 1), F32)
    for i in range(2):
        number = ids_ref[:, i : i + 1].astype(jnp.int32)
        total += jnp.sum(jnp.where(lane == number, probs, 0.0), axis=1, keepdims=True)
    own = jnp.sum(jnp.where(lane == expert, probs, 0.0), axis=1, keepdims=True)
    share_ref[...] = jnp.broadcast_to(own / total, share_ref.shape)
    x = x_ref[...]
    gate = nn(x, gate_ref[0])
    up = nn(x, up_ref[0])
    out_ref[...] = (gate * (1.0 / (1.0 + jnp.exp(-gate))) * up).astype(BF16)
    copy.wait()


def expert_out_kernel(seqs, held, w_ref, share_ref, *refs):
    h_refs, out_refs, acc_ref = refs[:seqs], refs[seqs : seqs + held], refs[seqs + held]
    part = h_refs[0].shape[-1]
    me, expert = lax.axis_index("seq"), lax.axis_index("exp")
    all_ref = refs[seqs + held + 1]
    for r in range(seqs):
        at = pl.multiple_of(lax.rem(me + seqs - r, seqs) * part, part)
        all_ref[:, pl.ds(at, part)] = h_refs[r][...]
    total = nn(all_ref[...], w_ref[0])
    acc_ref[...] = total * share_ref[:, 0:1]
    for r in range(held):
        at = pl.multiple_of(lax.rem(expert + r, seqs) * CAP, CAP)
        out_refs[r][...] = acc_ref[pl.ds(at, CAP), :].astype(BF16)


def mixed_kernel(heads, seqs, grown_ref, local_ref, res_ref, again_ref, *refs):
    prefixes, mixed_ref = refs[:seqs], refs[seqs]
    me = lax.axis_index("seq")
    per = heads // seqs
    for r in range(seqs):
        share = lax.rem(me + seqs - r, seqs)
        for j in range(per):
            h = share * per + j
            cols = pl.ds(pl.multiple_of(h * HEAD, HEAD), HEAD)
            inter = nn(grown_ref[:, cols], prefixes[r][j * HEAD : (j + 1) * HEAD, :])
            attended = local_ref[:, cols] + inter
            power = jnp.mean(attended * attended, axis=1, keepdims=True)
            normed = attended * lax.rsqrt(power + EPS) * again_ref[pl.ds(h, 1), :]
            mixed_ref[:, cols] = (res_ref[:, cols].astype(F32) + normed).astype(BF16)


def add_kernel(held, mixed_ref, place_ref, *refs):
    y_refs, out_ref, y_ref = refs[:held], refs[held], refs[held + 1]
    me = lax.axis_index("seq")
    for r, ref in enumerate(y_refs):
        at = pl.multiple_of(lax.rem(me + held - r, held) * CAP, CAP)
        y_ref[pl.ds(at, CAP), :] = ref[...].astype(F32)
    extra = tn(place_ref[...].astype(BF16), y_ref[...].astype(BF16))
    out_ref[...] = (mixed_ref[...].astype(F32) + extra).astype(BF16)


def run(body, out_shape, args, scratch=(), flops=1000, nbytes=1000, vmem=SMALL, anywhere=0):
    outs = out_shape if isinstance(out_shape, tuple) else (out_shape,)
    specs = tuple(VMEM for _ in outs)
    kernel = pl.pallas_call(
        body,
        out_shape=out_shape,
        in_specs=[VMEM] * (len(args) - anywhere) + [pl.BlockSpec(memory_space=pltpu.HBM)] * anywhere,
        out_specs=specs if isinstance(out_shape, tuple) else specs[0],
        scratch_shapes=list(scratch),
        compiler_params=pltpu.CompilerParams(vmem_limit_bytes=vmem),
        cost_estimate=pl.CostEstimate(flops=flops, bytes_accessed=nbytes, transcendentals=0),
    )
    near = len(args) - anywhere
    return kernel(*args[:near], *(pltpu.with_memory_space_constraint(x, pltpu.HBM) for x in args[near:]))


def spread(pieces, axis, count):
    parts = [pieces[0]]
    for r in range(1, count):
        parts.append(lax.ppermute(pieces[r], axis, [(i, (i + r) % count) for i in range(count)]))
    return parts


def ring_body(
    residual, query_rows, key_rows, value_rows, log_decay, attn_gain, norm_gain, router, expert_ids, priority,
    gate_weight, up_weight, down_weight,
):
    rows, width = residual.shape
    heads = width // HEAD
    held = lax.axis_size("exp")
    seqs = lax.axis_size("seq")
    experts = router.shape[1]
    part = width // seqs
    slot_rows = seqs * CAP
    hidden_part = gate_weight.shape[2]
    out_part = down_weight.shape[2]
    small = (
        key_rows, value_rows, log_decay.T, query_rows, residual, expert_ids.T, priority, router.T,
        norm_gain.reshape(heads, HEAD), attn_gain.reshape(heads, HEAD),
    )
    *outs, cum_row, cum_col = run(
        functools.partial(state_pieces_kernel, heads, seqs, len(small)),
        (
            *(pltpu.VMEM(x.shape, x.dtype) for x in small),
            *(shaped((part + PAD, LANES), BF16) for _ in range(seqs)),
            shaped((LANES, rows), F32),
            shaped((rows, LANES), F32),
        ),
        small,
        scratch=[
            pltpu.VMEM((LANES, rows), F32),
            pltpu.VMEM((LANES, rows), F32),
            pltpu.SemaphoreType.DMA((len(small),)),
        ],
        anywhere=len(small),
    )
    keys, values, _, queries, stream, ids, order, router_rows, gain, again = outs[: len(small)]
    pieces = outs[len(small) :]
    states = spread(pieces, "seq", seqs)
    table = run(functools.partial(pack_kernel, heads), shaped((experts + PAD, width), BF16), (router_rows, gain))
    tables = spread([table] * held, "exp", held)
    local, grown, place, *row_pieces = run(
        functools.partial(rows_kernel, heads, seqs, held),
        (
            shaped((rows, width), F32),
            shaped((rows, width), BF16),
            shaped((held * CAP, rows), F32),
            *(shaped((held * CAP, 3 * part + LANES), BF16) for _ in range(seqs)),
        ),
        (queries, keys, values, stream, cum_row, cum_col, ids, order),
        flops=200_000_000,
        nbytes=2_000_000,
    )
    row_parts = spread(row_pieces, "seq", seqs)
    (gate_kept,) = run(
        functools.partial(keep_kernel, (0,)),
        (pltpu.VMEM(gate_weight.shape, BF16),),
        (row_pieces[0], gate_weight),
        scratch=[pltpu.SemaphoreType.DMA((1,))],
        nbytes=14_000_000,
        anywhere=1,
    )
    *outs, slot_ids = run(
        functools.partial(owner_kernel, heads, seqs, held),
        (
            *(shaped((slot_rows, part), BF16) for _ in range(held)),
            shaped((slot_rows, LANES), F32),
            *(shaped((part, LANES), BF16) for _ in range(seqs)),
        ),
        (again, *states, *row_parts),
        scratch=[
            pltpu.VMEM((seqs, part + PAD, LANES), BF16),
            pltpu.VMEM((seqs, held * CAP, 3 * part + LANES), BF16),
            pltpu.VMEM((seqs, part, LANES), BF16),
            pltpu.VMEM((seqs, held * CAP, part), F32),
        ],
    )
    slots, slot_ids, prefixes = outs[:held], outs[held], outs[held + 1 :] + [slot_ids]
    swapped = run(join_kernel, shaped((held, slot_rows, part), BF16), spread(slots, "exp", held))
    gathered = spread([swapped] * seqs, "seq", seqs)
    (up_kept,) = run(
        functools.partial(keep_kernel, (0,)),
        (pltpu.VMEM(up_weight.shape, BF16),),
        (swapped, up_weight),
        scratch=[pltpu.SemaphoreType.DMA((1,))],
        nbytes=14_000_000,
        anywhere=1,
    )
    hidden, shares, down_kept = run(
        functools.partial(expert_in_kernel, seqs, held, width),
        (
            shaped((slot_rows, hidden_part), BF16),
            shaped((slot_rows, LANES), F32),
            pltpu.VMEM(down_weight.shape, BF16),
        ),
        (slot_ids, gate_kept, up_kept, *gathered, *tables, down_weight),
        scratch=[pltpu.VMEM((slot_rows, held * width), BF16), pltpu.SemaphoreType.DMA],
        flops=900_000_000,
        nbytes=28_000_000,
        anywhere=1,
    )
    hiddens = spread([hidden] * seqs, "seq", seqs)
    returned = spread(prefixes, "seq", seqs)
    outs = run(
        functools.partial(expert_out_kernel, seqs, held),
        (shaped((CAP, out_part), BF16),) * held,
        (down_kept, shares, *hiddens),
        scratch=[pltpu.VMEM((slot_rows, out_part), F32), pltpu.VMEM((slot_rows, seqs * hidden_part), BF16)],
        flops=450_000_000,
        nbytes=14_000_000,
    )
    y = [
        lax.ppermute(
            piece,
            ("seq", "exp"),
            [(s * held + e, ((e + r) % seqs) * held + s) for s in range(seqs) for e in range(held)],
        )
        for r, piece in enumerate(outs)
    ]
    mixed = run(
        functools.partial(mixed_kernel, heads, seqs),
        shaped((rows, width), BF16),
        (grown, local, stream, again, *returned),
        flops=100_000_000,
        nbytes=2_000_000,
    )
    return run(
        functools.partial(add_kernel, held),
        shaped((rows, width), BF16),
        (mixed, place, *y),
        scratch=[pltpu.VMEM((held * CAP, width), F32)],
    )


def body(residual, *args):
    seqs, held = lax.axis_size("seq"), lax.axis_size("exp")
    if seqs == held and (residual.shape[1] // HEAD) % seqs == 0:
        return ring_body(residual, *args)
    return general_body(residual, *args)


def solution(mesh):
    token = P(("groups", "seq"), "exp")
    return jax.shard_map(
        body,
        mesh=mesh,
        in_specs=(
            token, token, token, token, token, P("exp"), P("exp"), P("exp", None),
            P(("groups", "seq"), None), P(("groups", "seq"), None),
            P("exp", None, "seq"), P("exp", None, "seq"), P("exp", None, "seq"),
        ),
        out_specs=token,
        check_vma=False,
    )
```

```python
import functools

import jax
import jax.numpy as jnp
from jax import lax
from jax.experimental import pallas as pl
from jax.experimental.pallas import tpu as pltpu
from jax.sharding import PartitionSpec as P


HEAD = 128
LANES = 128
CAP = 8
PAD = 16
EPS = 1e-06
SMALL = 8 << 20
F32 = jnp.float32
BF16 = jnp.bfloat16


VMEM = pl.BlockSpec(memory_space=pltpu.VMEM)


def nt(a, b):
    return lax.dot_general(a, b, (((1,), (1,)), ((), ())), preferred_element_type=F32)


def tn(a, b):
    return lax.dot_general(a, b, (((0,), (0,)), ((), ())), preferred_element_type=F32)


def nn(a, b):
    return lax.dot_general(a, b, (((1,), (0,)), ((), ())), preferred_element_type=F32)


def iota(shape, dim):
    return lax.broadcasted_iota(jnp.int32, shape, dim)


def split_hi_lo(x):
    hi = x.astype(BF16)
    return hi, (x - hi.astype(F32)).astype(BF16)


def state_kernel(heads, shares, share_rows, k_ref, v_ref, decay_ref, pay_ref, row_ref, col_ref, pad_ref):
    rows = k_ref.shape[0]
    pad_ref[...] = jnp.zeros_like(pad_ref)
    pad_ref[0:heads, :] = decay_ref[...]
    log_decay = pad_ref[...]
    lower = jnp.where(iota((rows, rows), 0) >= iota((rows, rows), 1), 1.0, 0.0).astype(F32)
    cum_col = lax.dot_general(
        lower, log_decay, (((1,), (1,)), ((), ())), precision=lax.Precision.HIGHEST, preferred_element_type=F32
    )
    cum_row = lax.dot_general(
        log_decay, lower, (((1,), (1,)), ((), ())), precision=lax.Precision.HIGHEST, preferred_element_type=F32
    )
    row_ref[...] = cum_row
    col_ref[...] = cum_col
    to_end = jnp.exp(cum_col[rows - 1 : rows, :] - cum_col)
    hi, lo = split_hi_lo(jnp.exp(cum_col[rows - 1 : rows, :]))
    for s in range(shares):
        pay_ref[s, share_rows : share_rows + PAD, :] = jnp.concatenate(
            [jnp.broadcast_to(hi, (8, LANES)), jnp.broadcast_to(lo, (8, LANES))], axis=0
        )
    for h in range(heads):
        cols = slice(h * HEAD, (h + 1) * HEAD)
        keyed = (k_ref[:, cols].astype(F32) * to_end[:, h : h + 1]).astype(BF16)
        state = tn(keyed, v_ref[:, cols]).astype(BF16)
        at = h * HEAD
        while at < (h + 1) * HEAD:
            share, inner = divmod(at, share_rows)
            take = min(share_rows - inner, (h + 1) * HEAD - at)
            pay_ref[share, inner : inner + take, :] = state[at - h * HEAD : at - h * HEAD + take, :]
            at += take


def local_kernel(heads, q_ref, k_ref, v_ref, row_ref, col_ref, out_ref):
    rows = q_ref.shape[0]
    causal = iota((rows, rows), 0) >= iota((rows, rows), 1)
    for h in range(heads):
        cols = slice(h * HEAD, (h + 1) * HEAD)
        scores = nt(q_ref[:, cols], k_ref[:, cols])
        spread = col_ref[:, h : h + 1] - row_ref[h : h + 1, :]
        weights = jnp.where(causal, scores * jnp.exp(jnp.where(causal, spread, 0.0)), 0.0).astype(BF16)
        out_ref[:, cols] = nn(weights, v_ref[:, cols])


def place_kernel(held, ids_ref, prio_ref, place_ref):
    rows = ids_ref.shape[1]
    order = prio_ref[...].astype(F32)
    across = jnp.broadcast_to(order, (rows, rows))
    earlier = jnp.where(across.T < across, 1.0, 0.0).astype(BF16)
    ids = ids_ref[...]
    expert = iota((8 * pl.cdiv(held, 8), rows), 0)
    hit = expert == ids[0:1, :]
    for i in range(1, ids.shape[0]):
        hit = hit | (expert == ids[i : i + 1, :])
    member = jnp.where(hit, 1.0, 0.0)
    rank = nn(member.astype(BF16), earlier)
    slot = iota((CAP, rows), 0).astype(F32)
    for e in range(held):
        chosen = (member[e : e + 1, :] > 0.5) & (rank[e : e + 1, :] == slot)
        place_ref[e * CAP : (e + 1) * CAP, :] = jnp.where(chosen, 1.0, 0.0)


def scan_kernel(shares, share_rows, in_ref, out_ref):
    me = lax.axis_index("seq")
    row = me * share_rows + iota((share_rows, LANES), 0)
    onehot = jnp.where(row // HEAD == iota((share_rows, LANES), 1), 1.0, 0.0)
    carry = jnp.zeros((share_rows, LANES), F32)
    for b in range(shares):
        out_ref[b, :, :] = carry.astype(BF16)
        if b + 1 < shares:
            tail = in_ref[b, share_rows : share_rows + PAD, :].astype(F32)
            decay = tail[0:1, :] + tail[8:9, :]
            each = jnp.sum(onehot * decay, axis=1, keepdims=True)
            carry = each * carry + in_ref[b, 0:share_rows, :].astype(F32)


def mix_kernel(
    heads, held, copies, q_ref, local_ref, carried_ref, col_ref, res_ref, again_ref, ngain_ref, router_ref, place_ref,
    mixed_ref, slots_ref, stats_ref,
):
    rows = q_ref.shape[0]
    width = heads * HEAD
    experts = router_ref.shape[0]
    place = place_ref[...].astype(BF16)
    grow = jnp.exp(col_ref[...])
    squares = jnp.zeros((rows, 1), F32)
    picked_squares = jnp.zeros((held * CAP, 1), F32)
    logits = jnp.zeros((experts, rows), F32)
    for h in range(heads):
        cols = slice(h * HEAD, (h + 1) * HEAD)
        inter = nn(q_ref[:, cols], carried_ref[h * HEAD : (h + 1) * HEAD, :])
        attended = local_ref[:, cols] + grow[:, h : h + 1] * inter
        power = jnp.mean(attended * attended, axis=1, keepdims=True)
        normed = attended * lax.rsqrt(power + EPS) * again_ref[:, cols]
        mixed = (res_ref[:, cols].astype(F32) + normed).astype(BF16)
        mixed_ref[:, cols] = mixed
        mixed_f = mixed.astype(F32)
        squares += jnp.sum(mixed_f * mixed_f, axis=1, keepdims=True)
        hi, lo = split_hi_lo(mixed_f * ngain_ref[:, cols])
        logits += nt(router_ref[:, cols], hi) + nt(router_ref[:, cols], lo)
        picked = nn(place, mixed)
        picked_squares += jnp.sum(picked * picked, axis=1, keepdims=True)
        sent = (picked * ngain_ref[:, cols]).astype(BF16)
        for s in range(copies):
            for e in range(held):
                slots_ref[s, e, :, cols] = sent[e * CAP : (e + 1) * CAP, :]
    lane = iota((held * CAP, LANES), 1)
    hi, lo = split_hi_lo(picked_squares)
    extra = jnp.where(lane == 0, hi.astype(F32), jnp.where(lane == 1, lo.astype(F32), 0.0)).astype(BF16)
    for s in range(copies):
        for e in range(held):
            slots_ref[s, e, :, width : width + LANES] = extra[e * CAP : (e + 1) * CAP, :]
    stats_ref[0:experts, :] = logits
    stats_ref[experts : experts + 8, :] = jnp.broadcast_to(squares, (rows, rows)).T[0:8, :]


def gate_up_kernel(seqs, held, width, chunk, in_ref, gate_ref, up_ref, out_ref, x_ref, acc_g, acc_u):
    step = pl.program_id(0)
    per = width // chunk

    @pl.when(step == 0)
    def _():
        for s in range(seqs):
            for k in range(held):
                for p in range(per):
                    x_ref[k * per + p, s * CAP : (s + 1) * CAP, :] = in_ref[s * held + k, :, p * chunk : (p + 1) * chunk]
        acc_g[...] = jnp.zeros_like(acc_g)
        acc_u[...] = jnp.zeros_like(acc_u)

    x = x_ref[step]
    acc_g[...] += nn(x, gate_ref[0])
    acc_u[...] += nn(x, up_ref[0])

    @pl.when(step == pl.num_programs(0) - 1)
    def _():
        parts = []
        for s in range(seqs):
            total = jnp.zeros((CAP, 1), F32)
            for k in range(held):
                tail = in_ref[s * held + k, :, width : width + LANES].astype(F32)
                total += tail[:, 0:1] + tail[:, 1:2]
            parts.append(total)
        squares = jnp.concatenate(parts, axis=0)
        inverse = lax.rsqrt(squares / (held * width) + EPS)
        gate = acc_g[...] * inverse
        up = acc_u[...] * inverse
        out_ref[...] = (gate * (1.0 / (1.0 + jnp.exp(-gate))) * up).astype(BF16)


def down_kernel(seqs, order_ref, h_ref, w_ref, out_ref, acc):
    step = pl.program_id(0)

    @pl.when(step == 0)
    def _():
        acc[...] = jnp.zeros_like(acc)

    acc[...] += nn(h_ref[0], w_ref[0])

    @pl.when(step == pl.num_programs(0) - 1)
    def _():
        for s in range(seqs):
            out_ref[s, :, :] = acc[s * CAP : (s + 1) * CAP, :].astype(BF16)


def gates_kernel(held, total_width, parts, *refs):
    stats_refs, (ids_ref, place_ref, hi_ref, lo_ref) = refs[:parts], refs[parts:]
    total = stats_refs[0][...]
    for ref in stats_refs[1:]:
        total = total + ref[...]
    experts = total.shape[0] - 8
    inverse = lax.rsqrt(total[experts : experts + 1, :] / total_width + EPS)
    logits = total[0:experts, :] * inverse
    probs = 1.0 / (1.0 + jnp.exp(-logits))
    expert = iota(probs.shape, 0)
    ids = ids_ref[...]
    chosen = [
        jnp.sum(jnp.where(expert == ids[i : i + 1, :], probs, 0.0), axis=0, keepdims=True) for i in range(ids.shape[0])
    ]
    norm = chosen[0]
    for c in chosen[1:]:
        norm = norm + c
    for e in range(held):
        gate = jnp.zeros_like(norm)
        for i, c in enumerate(chosen):
            gate += jnp.where(ids[i : i + 1, :] == e, c / norm, 0.0)
        hi, lo = split_hi_lo(place_ref[e * CAP : (e + 1) * CAP, :] * gate)
        hi_ref[e * CAP : (e + 1) * CAP, :] = hi.astype(F32)
        lo_ref[e * CAP : (e + 1) * CAP, :] = lo.astype(F32)


def combine_kernel(held, mixed_ref, hi_ref, lo_ref, *refs):
    y_refs, out_ref = refs[:-1], refs[-1]
    if len(y_refs) > 1:
        y = jnp.concatenate([r[...].astype(F32) for r in y_refs], axis=0).astype(BF16)
    else:
        y = jnp.concatenate([y_refs[0][e].astype(F32) for e in range(held)], axis=0).astype(BF16)
    extra = tn(hi_ref[...].astype(BF16), y) + tn(lo_ref[...].astype(BF16), y)
    out_ref[...] = (mixed_ref[...].astype(F32) + extra).astype(BF16)


def call(body, out_shape, args, scratch=(), flops=0, nbytes=0):
    return pl.pallas_call(
        body,
        out_shape=out_shape,
        in_specs=[VMEM] * len(args),
        out_specs=jax.tree.map(lambda _: VMEM, out_shape),
        scratch_shapes=list(scratch),
        cost_estimate=pl.CostEstimate(flops=flops or 1000, bytes_accessed=nbytes or 1000, transcendentals=0),
    )(*args)


def shaped(shape, dtype):
    return jax.ShapeDtypeStruct(shape, dtype)


def general_body(
    residual, query_rows, key_rows, value_rows, log_decay, attn_gain, norm_gain, router, expert_ids, priority,
    gate_weight, up_weight, down_weight,
):
    rows, width = residual.shape
    heads = width // HEAD
    held = lax.axis_size("exp")
    seqs = lax.axis_size("seq")
    experts = router.shape[1]
    share_rows = width // seqs
    hidden_part = gate_weight.shape[2]
    out_part = down_weight.shape[2]
    ids = expert_ids.T
    payload, cum_row, cum_col = call(
        functools.partial(state_kernel, heads, seqs, share_rows),
        (
            shaped((seqs, share_rows + PAD, LANES), BF16),
            shaped((LANES, rows), F32),
            shaped((rows, LANES), F32),
        ),
        (key_rows, value_rows, log_decay.T),
        scratch=[pltpu.VMEM((LANES, rows), F32)],
        flops=60_000_000,
        nbytes=1_200_000,
    )
    arrived = lax.all_to_all(payload, "seq", split_axis=0, concat_axis=0, tiled=True)
    local = call(
        functools.partial(local_kernel, heads),
        shaped((rows, width), F32),
        (query_rows, key_rows, value_rows, cum_row, cum_col),
        flops=200_000_000,
        nbytes=2_000_000,
    )
    place = call(functools.partial(place_kernel, held), shaped((held * CAP, rows), F32), (ids, priority))
    prefix = call(functools.partial(scan_kernel, seqs, share_rows), shaped((seqs, share_rows, LANES), BF16), (arrived,))
    carried = lax.all_to_all(prefix, "seq", split_axis=0, concat_axis=0, tiled=True).reshape(width, LANES)
    mixed, slots, stats = call(
        functools.partial(mix_kernel, heads, held, seqs),
        (
            shaped((rows, width), BF16),
            shaped((seqs, held, CAP, width + LANES), BF16),
            shaped((experts + 8, rows), F32),
        ),
        (
            query_rows, local, carried, cum_col, residual, attn_gain[None], norm_gain[None], router.T, place,
        ),
        flops=200_000_000,
        nbytes=3_000_000,
    )
    slots = slots.reshape(seqs * held, CAP, width + LANES)
    gathered = lax.all_to_all(slots, ("seq", "exp"), split_axis=0, concat_axis=0, tiled=True)
    stat_parts = [stats]
    for r in range(1, held):
        stat_parts.append(lax.ppermute(stats, "exp", [(i, (i + r) % held) for i in range(held)]))
    slot_rows = seqs * CAP
    chunk = width // 2
    hidden = pl.pallas_call(
        functools.partial(gate_up_kernel, seqs, held, width, chunk),
        out_shape=shaped((slot_rows, hidden_part), BF16),
        grid=(held * width // chunk,),
        in_specs=[
            VMEM,
            pl.BlockSpec((1, chunk, hidden_part), lambda i: (0, i, 0)),
            pl.BlockSpec((1, chunk, hidden_part), lambda i: (0, i, 0)),
        ],
        out_specs=pl.BlockSpec((slot_rows, hidden_part), lambda i: (0, 0)),
        scratch_shapes=[
            pltpu.VMEM((held * width // chunk, slot_rows, chunk), BF16),
            pltpu.VMEM((slot_rows, hidden_part), F32),
            pltpu.VMEM((slot_rows, hidden_part), F32),
        ],
        name="gate_up",
        cost_estimate=pl.CostEstimate(flops=900_000_000, bytes_accessed=28_000_000, transcendentals=0),
    )(gathered, gate_weight, up_weight)
    me = lax.axis_index("seq")
    if seqs <= 8:
        parts = [hidden]
        for r in range(1, seqs):
            parts.append(lax.ppermute(hidden, "seq", [(i, (i + r) % seqs) for i in range(seqs)]))
        whole = jnp.stack(parts)
        order = jnp.mod(me - jnp.arange(seqs, dtype=jnp.int32), seqs)
    else:
        whole = lax.all_gather(hidden, "seq", axis=0)
        order = jnp.arange(seqs, dtype=jnp.int32)
    expert_out = pl.pallas_call(
        functools.partial(down_kernel, seqs),
        out_shape=shaped((seqs, CAP, out_part), BF16),
        grid_spec=pltpu.PrefetchScalarGridSpec(
            num_scalar_prefetch=1,
            grid=(seqs,),
            in_specs=[
                pl.BlockSpec((1, slot_rows, hidden_part), lambda i, o: (i, 0, 0)),
                pl.BlockSpec((1, hidden_part, out_part), lambda i, o: (0, o[i], 0)),
            ],
            out_specs=pl.BlockSpec((seqs, CAP, out_part), lambda i, o: (0, 0, 0)),
            scratch_shapes=[pltpu.VMEM((slot_rows, out_part), F32)],
        ),
        name="down",
        cost_estimate=pl.CostEstimate(flops=450_000_000, bytes_accessed=14_000_000, transcendentals=0),
    )(order, whole, down_weight)
    if seqs == held:
        pieces = []
        for r in range(seqs):
            target = [
                (s * held + e, ((e + r) % seqs) * held + s) for s in range(seqs) for e in range(held)
            ]
            mine = lax.dynamic_index_in_dim(
                expert_out, jnp.mod(lax.axis_index("exp") + r, seqs), axis=0, keepdims=False
            )
            pieces.append(lax.ppermute(mine, ("seq", "exp"), target))
        stacked = jnp.stack(pieces)
        source = jnp.mod(me - jnp.arange(held, dtype=jnp.int32), held)
        y = (jnp.take(stacked, source, axis=0),)
    else:
        returned = lax.all_to_all(expert_out, "seq", split_axis=0, concat_axis=1, tiled=True)
        returned = returned.reshape(CAP, seqs * out_part)
        y = (lax.all_to_all(returned[None], "exp", split_axis=2, concat_axis=0, tiled=True),)
    hi, lo = call(
        functools.partial(gates_kernel, held, held * width, len(stat_parts)),
        (shaped((held * CAP, rows), F32),) * 2,
        (*stat_parts, ids, place),
    )
    return call(functools.partial(combine_kernel, held), shaped((rows, width), BF16), (mixed, hi, lo, *y))


def state_pieces_kernel(heads, seqs, count, *refs):
    sources, kept, refs = refs[:count], refs[count : 2 * count], refs[2 * count :]
    pieces, row_ref, col_ref, pad_ref, end_ref, sems = refs[:seqs], *refs[seqs:]
    copies = [pltpu.make_async_copy(a, b, sems.at[i]) for i, (a, b) in enumerate(zip(sources, kept))]
    for copy in copies:
        copy.start()
    k_ref, v_ref, decay_ref = kept[:3]
    copies[2].wait()
    rows = k_ref.shape[0]
    per = heads // seqs
    me = lax.axis_index("seq")
    pad_ref[...] = jnp.zeros_like(pad_ref)
    pad_ref[0:heads, :] = decay_ref[...]
    log_decay = pad_ref[...]
    lower = jnp.where(iota((rows, rows), 0) >= iota((rows, rows), 1), 1.0, 0.0).astype(F32)
    cum_col = lax.dot_general(
        lower, log_decay, (((1,), (1,)), ((), ())), precision=lax.Precision.HIGHEST, preferred_element_type=F32
    )
    cum_row = lax.dot_general(
        log_decay, lower, (((1,), (1,)), ((), ())), precision=lax.Precision.HIGHEST, preferred_element_type=F32
    )
    row_ref[...] = cum_row
    col_ref[...] = cum_col
    end_ref[...] = jnp.exp(cum_row[:, rows - 1 : rows] - cum_row)
    hi, lo = split_hi_lo(jnp.exp(cum_col[rows - 1 : rows, :]))
    tail = jnp.concatenate([jnp.broadcast_to(hi, (8, LANES)), jnp.broadcast_to(lo, (8, LANES))], axis=0)
    copies[0].wait()
    copies[1].wait()
    for r in range(seqs):
        share = lax.rem(me + r, seqs)
        for j in range(per):
            h = share * per + j
            cols = pl.ds(pl.multiple_of(h * HEAD, HEAD), HEAD)
            keyed = (k_ref[:, cols].astype(F32).T * end_ref[pl.ds(h, 1), :]).astype(BF16)
            pieces[r][j * HEAD : (j + 1) * HEAD, :] = nn(keyed, v_ref[:, cols]).astype(BF16)
        pieces[r][per * HEAD : per * HEAD + PAD, :] = tail
    for copy in copies[3:]:
        copy.wait()


def pack_kernel(heads, router_ref, gain_ref, out_ref):
    experts = router_ref.shape[0]
    out_ref[0:experts, :] = router_ref[...]
    hi, lo = split_hi_lo(gain_ref[...])
    hi, lo = hi.astype(F32), lo.astype(F32)
    at = iota((PAD, HEAD), 0)
    for h in range(heads):
        both = jnp.where(at == 0, hi[h : h + 1, :], jnp.where(at == 1, lo[h : h + 1, :], 0.0))
        out_ref[experts : experts + PAD, h * HEAD : (h + 1) * HEAD] = both.astype(BF16)


def rows_kernel(
    heads, seqs, held, q_ref, k_ref, v_ref, res_ref, row_ref, col_ref, ids_ref, prio_ref, local_ref,
    grown_ref, place_ref, *pieces,
):
    place_kernel(held, ids_ref, prio_ref, place_ref)
    rows = q_ref.shape[0]
    causal = iota((rows, rows), 0) >= iota((rows, rows), 1)
    grow = jnp.exp(col_ref[...])
    for h in range(heads):
        cols = slice(h * HEAD, (h + 1) * HEAD)
        q = q_ref[:, cols]
        scores = nt(q, k_ref[:, cols])
        spread = col_ref[:, h : h + 1] - row_ref[h : h + 1, :]
        near = jnp.where(causal, scores * jnp.exp(jnp.where(causal, spread, 0.0)), 0.0).astype(BF16)
        local_ref[:, cols] = nn(near, v_ref[:, cols])
        grown_ref[:, cols] = (q.astype(F32) * grow[:, h : h + 1]).astype(BF16)
    place = place_ref[...]
    ids = ids_ref[...].astype(F32)
    lane = iota((held * CAP, LANES), 1)
    extra = jnp.zeros((held * CAP, LANES), F32)
    for i in range(ids.shape[0]):
        extra = jnp.where(lane == i, jnp.sum(place * ids[i : i + 1, :], axis=1, keepdims=True), extra)
    place = place.astype(BF16)
    me = lax.axis_index("seq")
    part = heads * HEAD // seqs
    for r in range(seqs):
        cols = pl.ds(pl.multiple_of(lax.rem(me + r, seqs) * part, part), part)
        pieces[r][:, 0:part] = nn(place, grown_ref[:, cols]).astype(BF16)
        pieces[r][:, part : 2 * part] = nn(place, local_ref[:, cols].astype(BF16)).astype(BF16)
        pieces[r][:, 2 * part : 3 * part] = nn(place, res_ref[:, cols]).astype(BF16)
        pieces[r][:, 3 * part : 3 * part + LANES] = extra.astype(BF16)


def copy_rows(source, start, target, sem):
    return pltpu.make_async_copy(source.at[:, pl.ds(start, target.shape[1]), :], target, sem)


def keep_kernel(starts, after_ref, *refs):
    count = len(starts)
    copies = [
        copy_rows(refs[i], starts[i], refs[count + i], refs[2 * count].at[i]) for i in range(count)
    ]
    for copy in copies:
        copy.start()
    for copy in copies:
        copy.wait()


def owner_kernel(heads, seqs, held, again_ref, *refs):
    states, rows_in = refs[:seqs], refs[seqs : 2 * seqs]
    slots_refs, ids_ref, *rest = refs[2 * seqs : 2 * seqs + held], *refs[2 * seqs + held :]
    prefixes, (state_ref, rows_ref, prefix_ref, mixed_ref) = rest[:seqs], rest[seqs:]
    per = heads // seqs
    part = per * HEAD
    me = lax.axis_index("seq")
    expert = lax.axis_index("exp")
    for r in range(seqs):
        b = lax.rem(me + seqs - r, seqs)
        state_ref[b] = states[r][...]
        rows_ref[b] = rows_in[r][...]
        mine = rows_in[r][:, 3 * part : 3 * part + LANES].astype(F32)
        picked = jnp.zeros((CAP, LANES), F32)
        for e in range(held):
            picked = jnp.where(expert == e, mine[e * CAP : (e + 1) * CAP, :], picked)
        ids_ref[pl.ds(pl.multiple_of(b * CAP, CAP), CAP), :] = picked
    lane = iota((1, LANES), 1)
    for j in range(per):
        h = me * per + j
        again = again_ref[pl.ds(h, 1), :]
        cols = slice(j * HEAD, (j + 1) * HEAD)
        carry = jnp.zeros((HEAD, HEAD), F32)
        for b in range(seqs):
            prefix = carry.astype(BF16)
            prefix_ref[b, cols, :] = prefix
            attended = rows_ref[b, :, part + j * HEAD : part + (j + 1) * HEAD].astype(F32)
            if b > 0:
                attended = attended + nn(rows_ref[b, :, cols], prefix)
            power = jnp.mean(attended * attended, axis=1, keepdims=True)
            normed = attended * lax.rsqrt(power + EPS) * again
            residual = rows_ref[b, :, 2 * part + j * HEAD : 2 * part + (j + 1) * HEAD].astype(F32)
            mixed_ref[b, :, cols] = residual + normed
            if b + 1 < seqs:
                tail = state_ref[b, part : part + PAD, :].astype(F32)
                decay = jnp.where(lane == h, tail[0:1, :] + tail[8:9, :], 0.0)
                carry = jnp.sum(decay, axis=1, keepdims=True) * carry + state_ref[b, cols, :].astype(F32)
    for r in range(held):
        at = pl.ds(pl.multiple_of(lax.rem(expert + r, held) * CAP, CAP), CAP)
        slots_refs[r][...] = jnp.concatenate([mixed_ref[b, at, :] for b in range(seqs)], axis=0).astype(BF16)
    for r in range(seqs):
        prefixes[r][...] = prefix_ref[lax.rem(me + r, seqs)]


def join_kernel(*refs):
    for r, ref in enumerate(refs[:-1]):
        refs[-1][r] = ref[...]


def expert_in_kernel(seqs, held, width, ids_ref, gate_ref, up_ref, *refs):
    gathered, tables, refs = refs[:seqs], refs[seqs : seqs + held], refs[seqs + held :]
    down_ref, out_ref, share_ref, kept_ref, x_ref, sem = refs
    copy = pltpu.make_async_copy(down_ref, kept_ref, sem)
    copy.start()
    slot_rows, part = gathered[0].shape[1:]
    experts = tables[0].shape[0] - PAD
    me, expert = lax.axis_index("seq"), lax.axis_index("exp")
    squares = jnp.zeros((slot_rows, 1), F32)
    for source in gathered:
        for r in range(held):
            piece = source[r].astype(F32)
            squares += jnp.sum(piece * piece, axis=1, keepdims=True)
    inverse = lax.rsqrt(squares / (held * width) + EPS)
    logits = jnp.zeros((slot_rows, experts), F32)
    for r in range(held):
        k = lax.rem(expert + held - r, held)
        for i in range(seqs):
            start = pl.multiple_of(lax.rem(me + seqs - i, seqs) * part, part)
            cols = pl.ds(start, part)
            gain = tables[r][experts : experts + PAD, cols].astype(F32)
            gain = gain[0:1, :] + gain[1:2, :]
            hi, lo = split_hi_lo(gathered[i][r].astype(F32) * gain * inverse)
            x_ref[:, pl.ds(pl.multiple_of(k * width + start, part), part)] = hi
            logits += nt(hi, tables[r][0:experts, cols]) + nt(lo, tables[r][0:experts, cols])
    probs = 1.0 / (1.0 + jnp.exp(-logits))
    lane = iota(probs.shape, 1)
    total = jnp.zeros((slot_rows, 1), F32)
    for i in range(2):
        number = ids_ref[:, i : i + 1].astype(jnp.int32)
        total += jnp.sum(jnp.where(lane == number, probs, 0.0), axis=1, keepdims=True)
    own = jnp.sum(jnp.where(lane == expert, probs, 0.0), axis=1, keepdims=True)
    share_ref[...] = jnp.broadcast_to(own / total, share_ref.shape)
    x = x_ref[...]
    gate = nn(x, gate_ref[0])
    up = nn(x, up_ref[0])
    out_ref[...] = (gate * (1.0 / (1.0 + jnp.exp(-gate))) * up).astype(BF16)
    copy.wait()


def down_part(me, seqs, steps, w_ref, h_refs):
    part = h_refs[0].shape[-1]
    total = None
    for r, h_ref in zip(steps, h_refs):
        at = pl.multiple_of(lax.rem(me + seqs - r, seqs) * part, part)
        term = nn(h_ref[...], w_ref[0, pl.ds(at, part), :])
        total = term if total is None else total + term
    return total


def expert_first_kernel(seqs, steps, w_ref, *refs):
    refs[-1][...] = down_part(lax.axis_index("seq"), seqs, steps, w_ref, refs[:-1])


def expert_out_kernel(seqs, held, steps, w_ref, share_ref, first_ref, *refs):
    count = len(steps)
    h_refs, out_refs, acc_ref = refs[:count], refs[count : count + held], refs[count + held]
    expert = lax.axis_index("exp")
    total = first_ref[...] + down_part(lax.axis_index("seq"), seqs, steps, w_ref, h_refs)
    acc_ref[...] = total * share_ref[:, 0:1]
    for r in range(held):
        at = pl.multiple_of(lax.rem(expert + r, seqs) * CAP, CAP)
        out_refs[r][...] = acc_ref[pl.ds(at, CAP), :].astype(BF16)


def mixed_kernel(heads, seqs, grown_ref, local_ref, res_ref, again_ref, *refs):
    prefixes, mixed_ref = refs[:seqs], refs[seqs]
    me = lax.axis_index("seq")
    per = heads // seqs
    for r in range(seqs):
        share = lax.rem(me + seqs - r, seqs)
        for j in range(per):
            h = share * per + j
            cols = pl.ds(pl.multiple_of(h * HEAD, HEAD), HEAD)
            inter = nn(grown_ref[:, cols], prefixes[r][j * HEAD : (j + 1) * HEAD, :])
            attended = local_ref[:, cols] + inter
            power = jnp.mean(attended * attended, axis=1, keepdims=True)
            normed = attended * lax.rsqrt(power + EPS) * again_ref[pl.ds(h, 1), :]
            mixed_ref[:, cols] = (res_ref[:, cols].astype(F32) + normed).astype(BF16)


def add_kernel(held, mixed_ref, place_ref, *refs):
    y_refs, out_ref, y_ref = refs[:held], refs[held], refs[held + 1]
    me = lax.axis_index("seq")
    for r, ref in enumerate(y_refs):
        at = pl.multiple_of(lax.rem(me + held - r, held) * CAP, CAP)
        y_ref[pl.ds(at, CAP), :] = ref[...].astype(F32)
    extra = tn(place_ref[...].astype(BF16), y_ref[...].astype(BF16))
    out_ref[...] = (mixed_ref[...].astype(F32) + extra).astype(BF16)


def run(body, out_shape, args, scratch=(), flops=1000, nbytes=1000, vmem=SMALL, anywhere=0):
    outs = out_shape if isinstance(out_shape, tuple) else (out_shape,)
    specs = tuple(VMEM for _ in outs)
    kernel = pl.pallas_call(
        body,
        out_shape=out_shape,
        in_specs=[VMEM] * (len(args) - anywhere) + [pl.BlockSpec(memory_space=pltpu.HBM)] * anywhere,
        out_specs=specs if isinstance(out_shape, tuple) else specs[0],
        scratch_shapes=list(scratch),
        compiler_params=pltpu.CompilerParams(vmem_limit_bytes=vmem),
        cost_estimate=pl.CostEstimate(flops=flops, bytes_accessed=nbytes, transcendentals=0),
    )
    near = len(args) - anywhere
    return kernel(*args[:near], *(pltpu.with_memory_space_constraint(x, pltpu.HBM) for x in args[near:]))


def spread(pieces, axis, count):
    parts = [pieces[0]]
    for r in range(1, count):
        parts.append(lax.ppermute(pieces[r], axis, [(i, (i + r) % count) for i in range(count)]))
    return parts


def ring_body(
    residual, query_rows, key_rows, value_rows, log_decay, attn_gain, norm_gain, router, expert_ids, priority,
    gate_weight, up_weight, down_weight,
):
    rows, width = residual.shape
    heads = width // HEAD
    held = lax.axis_size("exp")
    seqs = lax.axis_size("seq")
    experts = router.shape[1]
    part = width // seqs
    slot_rows = seqs * CAP
    hidden_part = gate_weight.shape[2]
    out_part = down_weight.shape[2]
    small = (
        key_rows, value_rows, log_decay.T, query_rows, residual, expert_ids.T, priority, router.T,
        norm_gain.reshape(heads, HEAD), attn_gain.reshape(heads, HEAD),
    )
    *outs, cum_row, cum_col = run(
        functools.partial(state_pieces_kernel, heads, seqs, len(small)),
        (
            *(pltpu.VMEM(x.shape, x.dtype) for x in small),
            *(shaped((part + PAD, LANES), BF16) for _ in range(seqs)),
            shaped((LANES, rows), F32),
            shaped((rows, LANES), F32),
        ),
        small,
        scratch=[
            pltpu.VMEM((LANES, rows), F32),
            pltpu.VMEM((LANES, rows), F32),
            pltpu.SemaphoreType.DMA((len(small),)),
        ],
        anywhere=len(small),
    )
    keys, values, _, queries, stream, ids, order, router_rows, gain, again = outs[: len(small)]
    pieces = outs[len(small) :]
    states = spread(pieces, "seq", seqs)
    table = run(functools.partial(pack_kernel, heads), shaped((experts + PAD, width), BF16), (router_rows, gain))
    tables = spread([table] * held, "exp", held)
    local, grown, place, *row_pieces = run(
        functools.partial(rows_kernel, heads, seqs, held),
        (
            shaped((rows, width), F32),
            shaped((rows, width), BF16),
            shaped((held * CAP, rows), F32),
            *(shaped((held * CAP, 3 * part + LANES), BF16) for _ in range(seqs)),
        ),
        (queries, keys, values, stream, cum_row, cum_col, ids, order),
        flops=200_000_000,
        nbytes=2_000_000,
    )
    row_parts = spread(row_pieces, "seq", seqs)
    (gate_kept,) = run(
        functools.partial(keep_kernel, (0,)),
        (pltpu.VMEM(gate_weight.shape, BF16),),
        (row_pieces[0], gate_weight),
        scratch=[pltpu.SemaphoreType.DMA((1,))],
        nbytes=14_000_000,
        anywhere=1,
    )
    *outs, slot_ids = run(
        functools.partial(owner_kernel, heads, seqs, held),
        (
            *(shaped((slot_rows, part), BF16) for _ in range(held)),
            shaped((slot_rows, LANES), F32),
            *(shaped((part, LANES), BF16) for _ in range(seqs)),
        ),
        (again, *states, *row_parts),
        scratch=[
            pltpu.VMEM((seqs, part + PAD, LANES), BF16),
            pltpu.VMEM((seqs, held * CAP, 3 * part + LANES), BF16),
            pltpu.VMEM((seqs, part, LANES), BF16),
            pltpu.VMEM((seqs, held * CAP, part), F32),
        ],
    )
    slots, slot_ids, prefixes = outs[:held], outs[held], outs[held + 1 :] + [slot_ids]
    swapped = run(join_kernel, shaped((held, slot_rows, part), BF16), spread(slots, "exp", held))
    gathered = spread([swapped] * seqs, "seq", seqs)
    (up_kept,) = run(
        functools.partial(keep_kernel, (0,)),
        (pltpu.VMEM(up_weight.shape, BF16),),
        (swapped, up_weight),
        scratch=[pltpu.SemaphoreType.DMA((1,))],
        nbytes=14_000_000,
        anywhere=1,
    )
    hidden, shares, down_kept = run(
        functools.partial(expert_in_kernel, seqs, held, width),
        (
            shaped((slot_rows, hidden_part), BF16),
            shaped((slot_rows, LANES), F32),
            pltpu.VMEM(down_weight.shape, BF16),
        ),
        (slot_ids, gate_kept, up_kept, *gathered, *tables, down_weight),
        scratch=[pltpu.VMEM((slot_rows, held * width), BF16), pltpu.SemaphoreType.DMA],
        flops=900_000_000,
        nbytes=28_000_000,
        anywhere=1,
    )
    hiddens = spread([hidden] * seqs, "seq", seqs)
    returned = spread(prefixes, "seq", seqs)
    early_steps = [0]
    late_steps = [r for r in range(seqs) if r not in early_steps]
    first = run(
        functools.partial(expert_first_kernel, seqs, early_steps),
        shaped((slot_rows, out_part), F32),
        (down_kept, *(hiddens[r] for r in early_steps)),
        flops=200_000_000,
        nbytes=7_000_000,
    )
    outs = run(
        functools.partial(expert_out_kernel, seqs, held, late_steps),
        (shaped((CAP, out_part), BF16),) * held,
        (down_kept, shares, first, *(hiddens[r] for r in late_steps)),
        scratch=[pltpu.VMEM((slot_rows, out_part), F32)],
        flops=200_000_000,
        nbytes=7_000_000,
    )
    y = [
        lax.ppermute(
            piece,
            ("seq", "exp"),
            [(s * held + e, ((e + r) % seqs) * held + s) for s in range(seqs) for e in range(held)],
        )
        for r, piece in enumerate(outs)
    ]
    mixed = run(
        functools.partial(mixed_kernel, heads, seqs),
        shaped((rows, width), BF16),
        (grown, local, stream, again, *returned),
        flops=100_000_000,
        nbytes=2_000_000,
    )
    return run(
        functools.partial(add_kernel, held),
        shaped((rows, width), BF16),
        (mixed, place, *y),
        scratch=[pltpu.VMEM((held * CAP, width), F32)],
    )


def body(residual, *args):
    seqs, held = lax.axis_size("seq"), lax.axis_size("exp")
    if seqs == held and (residual.shape[1] // HEAD) % seqs == 0:
        return ring_body(residual, *args)
    return general_body(residual, *args)


def solution(mesh):
    token = P(("groups", "seq"), "exp")
    return jax.shard_map(
        body,
        mesh=mesh,
        in_specs=(
            token, token, token, token, token, P("exp"), P("exp"), P("exp", None),
            P(("groups", "seq"), None), P(("groups", "seq"), None),
            P("exp", None, "seq"), P("exp", None, "seq"), P("exp", None, "seq"),
        ),
        out_specs=token,
        check_vma=False,
    )
```
